32 devices in a mesh: groups: 2 (over x), seq: 16 (over z, y, core).
Axes of the slice: x: 2, y: 2, z: 4, core: 2. Of those that a mesh axis runs over, the one named last changes fastest.
Arguments:
- queries: bfloat16 [8192, 256], P(('groups', 'seq')), parts along dimension 0, may hold values from -10 to 10
- key_vectors: bfloat16 [8192, 256], P(('groups', 'seq')), parts along dimension 0, may hold values from -10 to 10
- value_vectors: bfloat16 [8192, 1024], P(('groups', 'seq')), parts along dimension 0, may hold values from -6 to 6
- output_grad: bfloat16 [8192, 1024], P(('groups', 'seq')), parts along dimension 0, may hold values from -6 to 6
- norm_gain: float32 [1024], replicated, may hold values from 0.5 to 1.5
Outputs:
- mixed_out: bfloat16 [8192, 1024], P(('groups', 'seq')), parts along dimension 0
- query_grad: bfloat16 [8192, 256], P(('groups', 'seq')), parts along dimension 0
- key_grad: bfloat16 [8192, 256], P(('groups', 'seq')), parts along dimension 0
- value_grad: bfloat16 [8192, 1024], P(('groups', 'seq')), parts along dimension 0
The draws below stay inside these ranges and needn't reach their ends.
There are 2 independent parts, one for each index of `groups`. The reference program is written for one: setup_inputs(seed, part) draws one part's arguments, and reference() takes and returns one part's arrays. A program takes and returns all parts, laid end to end along the dimension named above; an argument that names none is the same for every part. Nothing has to cross between parts.
All inputs are finite; a program needn't handle non-finite values.
Results may differ from the reference program's by a relative error of at most 0.017.
Values may be sent and summed in bfloat16 or wider, within the bound.
A program may use at most 128 MiB of HBM per device.

```python
import jax
import jax.numpy as jnp
from jax import lax

H = 16
FD = 16
DV = 64
WIN = 64
BLK = 256
FEAT = 273
TOKENS = 4096


def paired_vectors(key, part):
    base_key = jax.random.fold_in(key, 7)
    array_shape = (TOKENS, H * FD)
    query_out = jnp.clip(jax.random.normal(jax.random.fold_in(base_key, 1), array_shape, jnp.float32), -6.0, 6.0)
    key_out = jnp.clip(jax.random.normal(jax.random.fold_in(base_key, 2), array_shape, jnp.float32), -6.0, 6.0)
    return (query_out, key_out)


def draw_queries(key, part):
    return paired_vectors(key, part)[0].astype(jnp.bfloat16)


def draw_key_vectors(key, part):
    return paired_vectors(key, part)[1].astype(jnp.bfloat16)


def levels(own_key, shape, shards, smallest, high):
    gain = 1.0
    for dim, shards_of in shards:
        draws = jax.random.uniform(jax.random.fold_in(jax.random.fold_in(own_key, 6), dim), (shards_of,), jnp.float32, smallest / len(shards), high / len(shards))
        gain = gain * jnp.repeat(jnp.exp(draws), shape[dim] // shards_of).reshape((-1,) + (1,) * (len(shape) - 1 - dim))
    return gain


def noise(rng, extent, scale, bound, cuts=(), held_as=jnp.bfloat16):
    array = scale * jax.random.normal(rng, extent, jnp.float32)
    if cuts:
        array = array * levels(rng, extent, cuts, -0.22, 0.18)
    return jnp.clip(array, -bound, bound).astype(held_as)


def setup_inputs(seed: int = 0, part: int = 0) -> dict:
    splits = jax.random.split(jax.random.key(seed), 6)
    part_splits = jax.random.split(jax.random.fold_in(splits[5], part), 6)
    queries = draw_queries(jax.random.fold_in(jax.random.fold_in(splits[5], part), 71), part)
    key_vectors = draw_key_vectors(jax.random.fold_in(jax.random.fold_in(splits[5], part), 71), part)
    value_vectors = noise(part_splits[2], (TOKENS, H * DV), 1.0, 6.0, ((0, 16),))
    output_grad = noise(part_splits[3], (TOKENS, H * DV), 1.0, 6.0, ((0, 16),))
    norm_gain = jnp.clip(1.0 + 0.1 * jax.random.normal(splits[4], (H * DV,), jnp.float32), 0.5, 1.5)
    return {"queries": queries, "key_vectors": key_vectors, "value_vectors": value_vectors, "output_grad": output_grad, "norm_gain": norm_gain}


quad_scale = 0.17677669529663687
epsilon = 1e-06
masked_score = -1e+30

def taylor_features(vectors, packed):
    row_count, head_count, feature_width = vectors.shape
    pieces = [jnp.ones((row_count, head_count, 1), jnp.float32), vectors * 0.5]
    if packed:
        for column in range(feature_width):
            factor = jnp.where(jnp.arange(feature_width - column) == 0, quad_scale, 0.25).astype(jnp.float32)
            pieces.append(vectors[:, :, column:column + 1] * vectors[:, :, column:] * factor)
    else:
        outer_product = vectors[:, :, :, None] * vectors[:, :, None, :]
        pieces.append(outer_product.reshape(row_count, head_count, feature_width * feature_width) * quad_scale)
    return jnp.concatenate(pieces, axis=-1)

def block_state(key_block, value_block, packed):
    row_count = key_block.shape[0]
    features = taylor_features(key_block.reshape(row_count, H, FD), packed)
    state_out = jnp.einsum('thf,the->fhe', features, value_block.reshape(row_count, H, DV), precision=lax.Precision.HIGHEST)
    return state_out.reshape(features.shape[-1], H * DV)

def mix_block(query_block, key_window, value_window, state_in, norm_gain, first_block):
    row_count = query_block.shape[0]
    key_span = key_window.shape[0]
    lookback = key_span - row_count
    packed = state_in.shape[0] != FEAT
    query_heads = query_block.reshape(row_count, H, FD)
    key_heads = key_window.reshape(key_span, H, FD)
    value_heads = value_window.reshape(key_span, H, DV)
    remote = jnp.einsum('thf,fhe->the', taylor_features(query_heads, packed), state_in.reshape(state_in.shape[0], H, DV), precision=lax.Precision.HIGHEST)
    query_half = query_heads.astype(jnp.bfloat16)
    key_half = key_heads.astype(jnp.bfloat16)
    value_half = value_heads.astype(jnp.bfloat16)
    scores = jnp.einsum('thd,uhd->htu', query_half, key_half, preferred_element_type=jnp.float32) * 0.25
    row_index = jnp.arange(row_count)[:, None]
    col_index = jnp.arange(key_span)[None, :]
    same_block = (col_index >= lookback) & (col_index - lookback <= row_index)
    kernel = jnp.where(same_block, 1.0 + scores + 0.5 * scores * scores, 0.0).astype(jnp.bfloat16)
    local_sum = jnp.einsum('htu,uhe->the', kernel, value_half, preferred_element_type=jnp.float32)
    numerator = remote + local_sum
    inverse_rms = lax.rsqrt(lax.optimization_barrier(jnp.mean(numerator * numerator, axis=-1, keepdims=True)) + epsilon)
    linear = numerator * inverse_rms * norm_gain.reshape(H, DV)
    inside = (col_index > row_index) & (col_index <= row_index + lookback) & jnp.logical_or(col_index >= lookback, jnp.logical_not(first_block))
    masked = jnp.where(inside, scores, masked_score)
    row_peak = lax.stop_gradient(lax.optimization_barrier(jnp.max(masked, axis=-1, keepdims=True)))
    weights = jnp.exp(masked - row_peak)
    weights_half = (weights / lax.optimization_barrier(jnp.sum(weights, axis=-1, keepdims=True))).astype(jnp.bfloat16)
    attended = jnp.einsum('htu,uhe->the', weights_half, value_half, preferred_element_type=jnp.float32)
    return (linear + attended).reshape(row_count, H * DV).astype(jnp.bfloat16)

def forward(query_full, key_full, value_full, norm_gain):
    blocks = TOKENS // BLK
    key_blocks = key_full.reshape(blocks, BLK, H * FD)
    value_blocks = value_full.reshape(blocks, BLK, H * DV)
    states = lax.map(jax.checkpoint(lambda operands: block_state(operands[0], operands[1], False)), (key_blocks, value_blocks))
    totals = jnp.cumsum(states, axis=0)
    prefixes = jnp.concatenate([jnp.zeros_like(states[:1]), totals[:-1]], axis=0)
    key_extended = jnp.concatenate([jnp.zeros((WIN, H * FD), jnp.float32), key_full], axis=0)
    value_extended = jnp.concatenate([jnp.zeros((WIN, H * DV), jnp.float32), value_full], axis=0)

    def one_block(operands):
        block_index, query_block, prefix = operands
        start = (block_index * BLK).astype(jnp.int32)
        key_window = lax.dynamic_slice_in_dim(key_extended, start, BLK + WIN, 0)
        value_window = lax.dynamic_slice_in_dim(value_extended, start, BLK + WIN, 0)
        return mix_block(query_block, key_window, value_window, prefix, norm_gain, block_index == 0)
    outputs = lax.map(jax.checkpoint(one_block), (jnp.arange(blocks, dtype=jnp.int32), query_full.reshape(blocks, BLK, H * FD), prefixes))
    return outputs.reshape(TOKENS, H * DV)

def reference(queries, key_vectors, value_vectors, output_grad, norm_gain):
    query_full = queries.astype(jnp.float32)
    key_full = key_vectors.astype(jnp.float32)
    value_full = value_vectors.astype(jnp.float32)
    mixed_out, pullback = jax.vjp(lambda first_arg, second_arg, third_arg: forward(first_arg, second_arg, third_arg, norm_gain), query_full, key_full, value_full)
    query_grad, key_grad, value_grad = pullback(output_grad)
    return (mixed_out, query_grad.astype(jnp.bfloat16), key_grad.astype(jnp.bfloat16), value_grad.astype(jnp.bfloat16))
```

```python
import functools

import jax
import jax.numpy as jnp
from jax import lax
from jax.experimental import pallas as pl
from jax.experimental.pallas import tpu as pltpu
from jax.sharding import PartitionSpec as P

H = 16
FD = 16
DV = 64
WIN = 64
BLK = 256
LANES = 128
MAIN = H * DV
PACKED = MAIN + MAIN // 4
QUAD = 0.17677669529663687
EPS = 1e-06
NEG = -1e30
F32 = jnp.float32
BF16 = jnp.bfloat16

NN = (((1,), (0,)), ((), ()))
NT = (((1,), (1,)), ((), ()))
TN = (((0,), (0,)), ((), ()))


def mm(a, b, dims=NN):
    return lax.dot_general(a, b, dims, preferred_element_type=F32)


def features(x):
    parts = [x * x * QUAD]
    for d in range(1, 8):
        parts.append(x * pltpu.roll(x, FD - d, 0) * 0.25)
    parts.append(x[:8] * x[8:] * 0.25)
    row = lax.broadcasted_iota(jnp.int32, (8, x.shape[1]), 0)
    parts.append(jnp.where(row == 0, 1.0, 0.0).astype(F32))
    parts.append(x * 0.5)
    return jnp.concatenate(parts, axis=0).astype(BF16)


def features_back(g, x):
    dx = (2.0 * QUAD) * g[:FD] * x
    for d in range(1, 8):
        part = g[d * FD : (d + 1) * FD] * 0.25
        dx = dx + part * pltpu.roll(x, FD - d, 0) + pltpu.roll(part * x, d, 0)
    half = g[128:136] * 0.25
    dx = dx + jnp.concatenate([half * x[8:], half * x[:8]], axis=0)
    return dx + 0.5 * g[144:160]


def turn(dst, src):
    for c in range(src.shape[1] // LANES):
        cols = slice(c * LANES, (c + 1) * LANES)
        dst[cols, :] = src[:, cols].T


def heads4(group, body):
    return [body(group * 4 + i, i) for i in range(4)]


def put_state(buf, group, states):
    for i, st in enumerate(states):
        buf[pl.ds(pl.multiple_of(group * 256 + i * 64, 64), 64), :] = st[:, :128].astype(BF16)
    rest = jnp.concatenate([st[:, 128:160] for st in states], axis=1)
    buf[pl.ds(pl.multiple_of(MAIN + group * 64, 64), 64), :] = rest.astype(BF16)


def get_state(buf, group, i):
    main = buf[pl.ds(pl.multiple_of(group * 256 + i * 64, 64), 64), :]
    rest = buf[pl.ds(pl.multiple_of(MAIN + group * 64, 64), 64), :][:, i * 32 : (i + 1) * 32]
    return main, rest


def qk_rows(h):
    return pl.ds(pl.multiple_of(h * FD, FD), FD)


def v_rows(h):
    return pl.ds(pl.multiple_of(h * DV, DV), DV)


def head_mask(rows, width, which):
    row = lax.broadcasted_iota(jnp.int32, (128, rows), 0)
    return (row >= which * width) & (row < (which + 1) * width)


def stage_state(k_ref, v_ref, kt_ref, vt_ref, state_ref):
    turn(kt_ref, k_ref)
    turn(vt_ref, v_ref)

    @pl.loop(0, H // 4)
    def _(group):
        def one(h, i):
            phi = features(kt_ref[qk_rows(h), :].astype(F32))
            return mm(vt_ref[v_rows(h), :], phi, NT)

        put_state(state_ref, group, heads4(group, one))


def tile_scores(kx, q_all, j, head8):
    zero = jnp.zeros_like(q_all)
    picked = jnp.where(head_mask(LANES, FD, head8), q_all, zero)
    return mm(kx, picked) * 0.25


def kernel_mask():
    r = lax.broadcasted_iota(jnp.int32, (128, 128), 0)
    c = lax.broadcasted_iota(jnp.int32, (128, 128), 1)
    return r <= c


def stage_local(q_ref, k_ref, v_ref, do_ref, kt_ref, vt_ref, rimk_ref, rimv_ref,
                qt_ref, dot_ref, num_ref, win_ref, dq_ref, dk_ref, dv_ref,
                kx, vx, ktx, vtx):
    turn(qt_ref, q_ref)
    turn(dot_ref, do_ref)
    kx[0:64, :] = jnp.zeros((64, H * FD), BF16)
    kx[64:128, :] = rimk_ref[...]
    kx[128:384, :] = k_ref[...]
    vx[0:64, :] = jnp.zeros((64, MAIN), BF16)
    vx[64:128, :] = rimv_ref[...]
    vx[128:384, :] = v_ref[...]
    for c in range(H * FD // LANES):
        cols = slice(c * LANES, (c + 1) * LANES)
        ktx[cols, 0:128] = kx[0:128, cols].T
    ktx[:, 128:384] = kt_ref[...]
    for c in range(MAIN // LANES):
        cols = slice(c * LANES, (c + 1) * LANES)
        vtx[cols, 0:128] = vx[0:128, cols].T
    vtx[:, 128:384] = vt_ref[...]
    first = lax.axis_index("seq") == 0
    lowest = jnp.where(first, 64, 0)
    r = lax.broadcasted_iota(jnp.int32, (192, 128), 0)
    c = lax.broadcasted_iota(jnp.int32, (192, 128), 1)
    band = (r >= c + 1) & (r <= c + 64)
    band0 = band & (r >= lowest)
    below = kernel_mask()
    for half in range(2):
        kcols = slice(half * LANES, (half + 1) * LANES)

        @pl.loop(0, 4)
        def _(pair, half=half, kcols=kcols):
            prow = pl.ds(pl.multiple_of(half * 512 + pair * LANES, LANES), LANES)
            for i in range(2):
                head8 = pair * 2 + i
                h = half * 8 + head8
                dks = []
                dvs = []
                for j in range(2):
                    cols = slice(j * 128, (j + 1) * 128)
                    keys = slice(j * 128, j * 128 + 256)
                    s = tile_scores(kx[keys, kcols], qt_ref[kcols, cols], j, head8)
                    kern = 1.0 + s + 0.5 * s * s
                    last = jnp.where(below, kern[128:], 0.0).astype(BF16)
                    if j == 0:
                        local = mm(vtx[v_rows(h), 128:256], last)
                    else:
                        local = mm(vtx[v_rows(h), 128:384],
                                   jnp.concatenate([kern[:128].astype(BF16), last], axis=0))
                    num_ref[v_rows(h), cols] = local
                    sw = jnp.where(band0 if j == 0 else band, s[64:], NEG)
                    e = jnp.exp(sw - jnp.max(sw, axis=0, keepdims=True))
                    p = e * (1.0 / jnp.sum(e, axis=0, keepdims=True))
                    w = p.astype(BF16)
                    pad = jnp.zeros((64, 128), BF16)
                    wide = jnp.concatenate([pad, w], axis=0)
                    win_ref[v_rows(h), cols] = mm(vtx[v_rows(h), keys], wide)
                    do_pair = dot_ref[prow, cols]
                    do_one = jnp.where(head_mask(LANES, DV, i), do_pair, jnp.zeros_like(do_pair))
                    vpair = vx[j * 128 + 64 : j * 128 + 256, pl.ds(pl.multiple_of(half * 512 + pair * LANES, LANES), LANES)]
                    dw = mm(vpair, do_one)
                    ds = p * (dw - jnp.sum(p * dw, axis=0, keepdims=True)) * 0.25
                    ds = jnp.concatenate([pad, ds.astype(BF16)], axis=0)
                    dq_ref[qk_rows(h), cols] = mm(ktx[qk_rows(h), keys], ds)
                    dks.append(mm(qt_ref[qk_rows(h), cols], ds, NT))
                    dvs.append(mm(dot_ref[v_rows(h), cols], wide, NT))
                for dst, rows, parts in ((dk_ref, qk_rows(h), dks), (dv_ref, v_rows(h), dvs)):
                    dst[rows, 0:128] = parts[0][:, :128]
                    dst[rows, 128:256] = parts[0][:, 128:] + parts[1][:, :128]
                    dst[rows, 256:384] = parts[1][:, 128:]


def stage_mix(prefix_ref, qt_ref, dot_ref, num_ref, win_ref, gain_ref,
              out_ref, dnum_ref, state_ref, outt):
    @pl.loop(0, H // 4)
    def _(group):
        def one(h, i):
            phi = features(qt_ref[qk_rows(h), :].astype(F32))
            main, rest = get_state(prefix_ref, group, i)
            num = num_ref[v_rows(h), :] + mm(main, phi[:128]) + mm(rest, phi[128:])
            inv = lax.rsqrt(jnp.mean(num * num, axis=0, keepdims=True) + EPS)
            gain = gain_ref[v_rows(h), :]
            unit = num * inv
            outt[v_rows(h), :] = (unit * gain + win_ref[v_rows(h), :]).astype(BF16)
            dg = dot_ref[v_rows(h), :].astype(F32) * gain
            dnum = inv * (dg - unit * jnp.mean(dg * unit, axis=0, keepdims=True))
            half = dnum.astype(BF16)
            dnum_ref[v_rows(h), :] = half
            return mm(half, phi, NT)

        put_state(state_ref, group, heads4(group, one))

    for c in range(MAIN // LANES):
        cols = slice(c * LANES, (c + 1) * LANES)
        out_ref[:, cols] = outt[cols, :].T


def stage_back(prefix_ref, qt_ref, kt_ref, k_ref, v_ref, dnum_ref, dq_in, dk_in, dv_in,
               qg_ref, dk_ref, dv_ref, dqt):
    below = kernel_mask()
    for half in range(2):
        kcols = slice(half * LANES, (half + 1) * LANES)

        @pl.loop(0, 2)
        def _(sub, half=half, kcols=kcols):
            group = half * 2 + sub
            for i in range(4):
                head8 = sub * 4 + i
                h = half * 8 + head8
                pcol = pl.ds(pl.multiple_of((group * 2 + i // 2) * LANES, LANES), LANES)
                dk = dk_in[qk_rows(h), 128:384]
                dv = dv_in[v_rows(h), 128:384]
                main, rest = get_state(prefix_ref, group, i)
                dnum = dnum_ref[v_rows(h), :]
                dphi = jnp.concatenate([mm(main, dnum, TN), mm(rest, dnum, TN)], axis=0)
                dq = dq_in[qk_rows(h), :] + features_back(dphi, qt_ref[qk_rows(h), :].astype(F32))
                dqs = []
                for j in range(2):
                    cols = slice(j * 128, (j + 1) * 128)
                    n = (j + 1) * 128
                    s = tile_scores(k_ref[:n, kcols], qt_ref[kcols, cols], j, head8)
                    dn_pair = dnum_ref[pcol, cols]
                    dn_one = jnp.where(head_mask(LANES, DV, i % 2), dn_pair, jnp.zeros_like(dn_pair))
                    dkern = mm(v_ref[:n, pcol], dn_one)
                    kern = 1.0 + s + 0.5 * s * s
                    ds = dkern * (0.25 + 0.25 * s)
                    if j == 0:
                        kern = jnp.where(below, kern, 0.0).astype(BF16)
                        ds = jnp.where(below, ds, 0.0).astype(BF16)
                    else:
                        kern = jnp.concatenate(
                            [kern[:128].astype(BF16), jnp.where(below, kern[128:], 0.0).astype(BF16)], axis=0)
                        ds = jnp.concatenate(
                            [ds[:128].astype(BF16), jnp.where(below, ds[128:], 0.0).astype(BF16)], axis=0)
                    dqs.append(mm(kt_ref[qk_rows(h), :n], ds))
                    dka = mm(qt_ref[qk_rows(h), cols], ds, NT)
                    dva = mm(dnum_ref[v_rows(h), cols], kern, NT)
                    if j == 0:
                        dka = jnp.concatenate([dka, jnp.zeros_like(dka)], axis=1)
                        dva = jnp.concatenate([dva, jnp.zeros_like(dva)], axis=1)
                    dk = dk + dka
                    dv = dv + dva
                dqt[qk_rows(h), :] = dq + jnp.concatenate(dqs, axis=1)
                dk_ref[qk_rows(h), :] = dk
                dv_ref[v_rows(h), :] = dv

    for c in range(H * FD // LANES):
        cols = slice(c * LANES, (c + 1) * LANES)
        qg_ref[:, cols] = dqt[cols, :].T.astype(BF16)


def stage_last(suffix_ref, kt_ref, vt_ref, dk_in, dv_in, rim_ref, kg_ref, vg_ref, dkt, dvt):
    @pl.loop(0, H // 4)
    def _(group):
        for i in range(4):
            h = group * 4 + i
            main, rest = get_state(suffix_ref, group, i)
            x = kt_ref[qk_rows(h), :].astype(F32)
            phi = features(x)
            vt = vt_ref[v_rows(h), :]
            dv = dv_in[v_rows(h), :] + mm(main, phi[:128]) + mm(rest, phi[128:])
            dphi = jnp.concatenate([mm(main, vt, TN), mm(rest, vt, TN)], axis=0)
            dk = dk_in[qk_rows(h), :] + features_back(dphi, x)
            rim_k = rim_ref[qk_rows(h), :].astype(F32)
            rim_v = rim_ref[pl.ds(pl.multiple_of(H * FD + h * DV, DV), DV), :].astype(F32)
            dkt[qk_rows(h), 0:128] = dk[:, :128]
            dkt[qk_rows(h), 128:256] = dk[:, 128:] + rim_k
            dvt[v_rows(h), 0:128] = dv[:, :128].astype(BF16)
            dvt[v_rows(h), 128:256] = (dv[:, 128:] + rim_v).astype(BF16)

    for c in range(H * FD // LANES):
        cols = slice(c * LANES, (c + 1) * LANES)
        kg_ref[:, cols] = dkt[cols, :].T.astype(BF16)
    for c in range(MAIN // LANES):
        cols = slice(c * LANES, (c + 1) * LANES)
        vg_ref[:, cols] = dvt[cols, :].T


def call(body, args, outs, scratch=(), flops=100_000_000):
    return pl.pallas_call(
        body,
        out_shape=[jax.ShapeDtypeStruct(s, d) for s, d in outs],
        in_specs=[pl.BlockSpec(memory_space=pltpu.VMEM)] * len(args),
        out_specs=[pl.BlockSpec(memory_space=pltpu.VMEM)] * len(outs),
        scratch_shapes=[pltpu.VMEM(s, d) for s, d in scratch],
        compiler_params=pltpu.CompilerParams(vmem_limit_bytes=56 * 1024 * 1024),
        cost_estimate=pl.CostEstimate(flops=flops, bytes_accessed=4_000_000, transcendentals=0),
    )(*args)


def passed_along(block, distance):
    devices = range(lax.axis_size("seq"))
    return lax.ppermute(block, "seq", [(i, i + distance) for i in devices if i + distance in devices])


def scan_states(state, reverse):
    n = lax.axis_size("seq")
    rows = -(-PACKED // n)
    padded = jnp.pad(state, ((0, rows * n - PACKED), (0, 0))).reshape(n, rows, LANES)
    parts = lax.all_to_all(padded, "seq", 0, 0).astype(F32)
    total = lax.cumsum(parts, axis=0, reverse=reverse)
    zero = jnp.zeros_like(total[:1])
    if reverse:
        sums = jnp.concatenate([total[1:], zero], axis=0)
    else:
        sums = jnp.concatenate([zero, total[:-1]], axis=0)
    back = lax.all_to_all(sums.astype(BF16), "seq", 0, 0)
    return back.reshape(n * rows, LANES)[:PACKED]


def on_device(q, k, v, do, gain):
    rim_k = passed_along(k[BLK - WIN :], 1)
    rim_v = passed_along(v[BLK - WIN :], 1)
    qk, vv = (H * FD, BLK), (MAIN, BLK)
    kt, vt, state = call(stage_state, (k, v), ((qk, BF16), (vv, BF16), ((PACKED, LANES), BF16)))
    prefix = scan_states(state, False)
    qt, dot, num, win, dq, dk, dv = call(
        stage_local, (q, k, v, do, kt, vt, rim_k, rim_v),
        ((qk, BF16), (vv, BF16), (vv, F32), (vv, F32), (qk, F32), ((H * FD, 384), F32), ((MAIN, 384), F32)),
        (((384, H * FD), BF16), ((384, MAIN), BF16), ((H * FD, 384), BF16), ((MAIN, 384), BF16)))
    rim = jnp.concatenate([dk[:, :128], dv[:, :128]], axis=0).astype(BF16)
    rim = passed_along(rim, -1)
    out, dnum, dstate = call(
        stage_mix, (prefix, qt, dot, num, win, gain.reshape(MAIN, 1)),
        (((BLK, MAIN), BF16), (vv, BF16), ((PACKED, LANES), BF16)), ((vv, BF16),))
    suffix = scan_states(dstate, True)
    qg, dk, dv = call(
        stage_back, (prefix, qt, kt, k, v, dnum, dq, dk, dv),
        (((BLK, H * FD), BF16), (qk, F32), (vv, F32)), ((qk, F32),))
    kg, vg = call(
        stage_last, (suffix, kt, vt, dk, dv, rim),
        (((BLK, H * FD), BF16), ((BLK, MAIN), BF16)), ((qk, F32), (vv, BF16)))
    return out, qg, kg, vg


def solution(mesh):
    split = P(("groups", "seq"), None)
    return jax.shard_map(
        on_device, mesh=mesh, in_specs=(split,) * 4 + (P(),), out_specs=(split,) * 4, check_vma=False
    )
```

```python
import functools

import jax
import jax.numpy as jnp
from jax import lax
from jax.experimental import pallas as pl
from jax.experimental.pallas import tpu as pltpu
from jax.sharding import PartitionSpec as P

H = 16
FD = 16
DV = 64
WIN = 64
BLK = 256
LANES = 128
MAIN = H * DV
PACKED = MAIN + MAIN // 4
QUAD = 0.17677669529663687
EPS = 1e-06
NEG = -1e30
F32 = jnp.float32
BF16 = jnp.bfloat16

NN = (((1,), (0,)), ((), ()))
NT = (((1,), (1,)), ((), ()))
TN = (((0,), (0,)), ((), ()))


def mm(a, b, dims=NN):
    return lax.dot_general(a, b, dims, preferred_element_type=F32)


def features(x):
    parts = [x * x * QUAD]
    for d in range(1, 8):
        parts.append(x * pltpu.roll(x, FD - d, 0) * 0.25)
    parts.append(x[:8] * x[8:] * 0.25)
    row = lax.broadcasted_iota(jnp.int32, (8, x.shape[1]), 0)
    parts.append(jnp.where(row == 0, 1.0, 0.0).astype(F32))
    parts.append(x * 0.5)
    return jnp.concatenate(parts, axis=0).astype(BF16)


def features_back(g, x):
    dx = (2.0 * QUAD) * g[:FD] * x
    for d in range(1, 8):
        part = g[d * FD : (d + 1) * FD] * 0.25
        dx = dx + part * pltpu.roll(x, FD - d, 0) + pltpu.roll(part * x, d, 0)
    half = g[128:136] * 0.25
    dx = dx + jnp.concatenate([half * x[8:], half * x[:8]], axis=0)
    return dx + 0.5 * g[144:160]


def turn(dst, src):
    for c in range(src.shape[1] // LANES):
        cols = slice(c * LANES, (c + 1) * LANES)
        dst[cols, :] = src[:, cols].T


def heads4(group, body):
    return [body(group * 4 + i, i) for i in range(4)]


def put_state(buf, group, states):
    for i, st in enumerate(states):
        buf[pl.ds(pl.multiple_of(group * 256 + i * 64, 64), 64), :] = st[:, :128].astype(BF16)
    rest = jnp.concatenate([st[:, 128:160] for st in states], axis=1)
    buf[pl.ds(pl.multiple_of(MAIN + group * 64, 64), 64), :] = rest.astype(BF16)


def get_state(buf, group, i):
    main = buf[pl.ds(pl.multiple_of(group * 256 + i * 64, 64), 64), :]
    rest = buf[pl.ds(pl.multiple_of(MAIN + group * 64, 64), 64), :][:, i * 32 : (i + 1) * 32]
    return main, rest


def qk_rows(h):
    return pl.ds(pl.multiple_of(h * FD, FD), FD)


def v_rows(h):
    return pl.ds(pl.multiple_of(h * DV, DV), DV)


def head_mask(rows, width, which):
    row = lax.broadcasted_iota(jnp.int32, (128, rows), 0)
    return (row >= which * width) & (row < (which + 1) * width)


def tile_scores(kx, q_all, j, head8):
    zero = jnp.zeros_like(q_all)
    picked = jnp.where(head_mask(LANES, FD, head8), q_all, zero)
    return mm(kx, picked) * 0.25


def kernel_mask():
    r = lax.broadcasted_iota(jnp.int32, (128, 128), 0)
    c = lax.broadcasted_iota(jnp.int32, (128, 128), 1)
    return r <= c


def stage_local(half, first, qt_ref, dot_ref, num_ref, win_ref, dq_ref, dk_ref, dv_ref, kx, vx, ktx, vtx):
    lowest = jnp.where(first, 64, 0)
    r = lax.broadcasted_iota(jnp.int32, (192, 128), 0)
    c = lax.broadcasted_iota(jnp.int32, (192, 128), 1)
    band = (r >= c + 1) & (r <= c + 64)
    band0 = band & (r >= lowest)
    below = kernel_mask()
    kcols = slice(half * LANES, (half + 1) * LANES)

    @pl.loop(0, 4)
    def _(pair):
        prow = pl.ds(pl.multiple_of(half * 512 + pair * LANES, LANES), LANES)
        for i in range(2):
            head8 = pair * 2 + i
            h = half * 8 + head8
            dks = []
            dvs = []
            for j in range(2):
                cols = slice(j * 128, (j + 1) * 128)
                keys = slice(j * 128, j * 128 + 256)
                s = tile_scores(kx[keys, kcols], qt_ref[kcols, cols], j, head8)
                kern = 1.0 + s + 0.5 * s * s
                last = jnp.where(below, kern[128:], 0.0).astype(BF16)
                if j == 0:
                    local = mm(vtx[v_rows(h), 128:256], last)
                else:
                    local = mm(vtx[v_rows(h), 128:384],
                               jnp.concatenate([kern[:128].astype(BF16), last], axis=0))
                num_ref[v_rows(h), cols] = local
                sw = jnp.where(band0 if j == 0 else band, s[64:], NEG)
                e = jnp.exp(sw - jnp.max(sw, axis=0, keepdims=True))
                p = e * (1.0 / jnp.sum(e, axis=0, keepdims=True))
                w = p.astype(BF16)
                pad = jnp.zeros((64, 128), BF16)
                wide = jnp.concatenate([pad, w], axis=0)
                win_ref[v_rows(h), cols] = mm(vtx[v_rows(h), keys], wide)
                do_pair = dot_ref[prow, cols]
                do_one = jnp.where(head_mask(LANES, DV, i), do_pair, jnp.zeros_like(do_pair))
                vpair = vx[j * 128 + 64 : j * 128 + 256, pl.ds(pl.multiple_of(half * 512 + pair * LANES, LANES), LANES)]
                dw = mm(vpair, do_one)
                ds = p * (dw - jnp.sum(p * dw, axis=0, keepdims=True)) * 0.25
                ds = jnp.concatenate([pad, ds.astype(BF16)], axis=0)
                dq_ref[qk_rows(h), cols] = mm(ktx[qk_rows(h), keys], ds)
                dks.append(mm(qt_ref[qk_rows(h), cols], ds, NT))
                dvs.append(mm(dot_ref[v_rows(h), cols], wide, NT))
            for dst, rows, parts in ((dk_ref, qk_rows(h), dks), (dv_ref, v_rows(h), dvs)):
                dst[rows, 0:128] = parts[0][:, :128]
                dst[rows, 128:256] = parts[0][:, 128:] + parts[1][:, :128]
                dst[rows, 256:384] = parts[1][:, 128:]


def stage_mix(prefix_ref, qt_ref, dot_ref, num_ref, win_ref, gain_ref,
              dnum_ref, state_ref, outt):
    @pl.loop(0, H // 4)
    def _(group):
        def one(h, i):
            phi = features(qt_ref[qk_rows(h), :].astype(F32))
            main, rest = get_state(prefix_ref, group, i)
            num = num_ref[v_rows(h), :] + mm(main, phi[:128]) + mm(rest, phi[128:])
            inv = lax.rsqrt(jnp.mean(num * num, axis=0, keepdims=True) + EPS)
            gain = jnp.concatenate([gain_ref[v_rows(h), :]] * 2, axis=1)
            unit = num * inv
            outt[v_rows(h), :] = (unit * gain + win_ref[v_rows(h), :]).astype(BF16)
            dg = dot_ref[v_rows(h), :].astype(F32) * gain
            dnum = inv * (dg - unit * jnp.mean(dg * unit, axis=0, keepdims=True))
            half = dnum.astype(BF16)
            dnum_ref[v_rows(h), :] = half
            return mm(half, phi, NT)

        put_state(state_ref, group, heads4(group, one))


def stage_back(half, prefix_ref, qt_ref, kt_ref, k_ref, v_ref, dnum_ref, dq_in, dk_in, dv_in, dqt):
    below = kernel_mask()
    kcols = slice(half * LANES, (half + 1) * LANES)
    dk_ref, dv_ref = dk_in, dv_in

    @pl.loop(0, 2)
    def _(sub):
        group = half * 2 + sub
        for i in range(4):
            head8 = sub * 4 + i
            h = half * 8 + head8
            pcol = pl.ds(pl.multiple_of((group * 2 + i // 2) * LANES, LANES), LANES)
            dk = dk_in[qk_rows(h), :]
            dv = dv_in[v_rows(h), :]
            main, rest = get_state(prefix_ref, group, i)
            dnum = dnum_ref[v_rows(h), :]
            dphi = jnp.concatenate([mm(main, dnum, TN), mm(rest, dnum, TN)], axis=0)
            dq = dq_in[qk_rows(h), :] + features_back(dphi, qt_ref[qk_rows(h), :].astype(F32))
            dqs = []
            for j in range(2):
                cols = slice(j * 128, (j + 1) * 128)
                n = (j + 1) * 128
                s = tile_scores(k_ref[:n, kcols], qt_ref[kcols, cols], j, head8)
                dn_pair = dnum_ref[pcol, cols]
                dn_one = jnp.where(head_mask(LANES, DV, i % 2), dn_pair, jnp.zeros_like(dn_pair))
                dkern = mm(v_ref[:n, pcol], dn_one)
                kern = 1.0 + s + 0.5 * s * s
                ds = dkern * (0.25 + 0.25 * s)
                if j == 0:
                    kern = jnp.where(below, kern, 0.0).astype(BF16)
                    ds = jnp.where(below, ds, 0.0).astype(BF16)
                else:
                    kern = jnp.concatenate(
                        [kern[:128].astype(BF16), jnp.where(below, kern[128:], 0.0).astype(BF16)], axis=0)
                    ds = jnp.concatenate(
                        [ds[:128].astype(BF16), jnp.where(below, ds[128:], 0.0).astype(BF16)], axis=0)
                dqs.append(mm(kt_ref[qk_rows(h), :n], ds))
                dka = mm(qt_ref[qk_rows(h), cols], ds, NT)
                dva = mm(dnum_ref[v_rows(h), cols], kern, NT)
                if j == 0:
                    dka = jnp.concatenate([dka, jnp.zeros_like(dka)], axis=1)
                    dva = jnp.concatenate([dva, jnp.zeros_like(dva)], axis=1)
                dk = dk + dka
                dv = dv + dva
            dqt[qk_rows(h), :] = dq + jnp.concatenate(dqs, axis=1)
            dk_ref[qk_rows(h), :] = dk
            dv_ref[v_rows(h), :] = dv


def stage_last(suffix_ref, kt_ref, vt_ref, dk_in, dv_in, rim_ref, kg_ref, vg_ref, dkt, dvt):
    @pl.loop(0, H // 4)
    def _(group):
        for i in range(4):
            h = group * 4 + i
            main, rest = get_state(suffix_ref, group, i)
            x = kt_ref[qk_rows(h), :].astype(F32)
            phi = features(x)
            vt = vt_ref[v_rows(h), :]
            dv = dv_in[v_rows(h), :] + mm(main, phi[:128]) + mm(rest, phi[128:])
            dphi = jnp.concatenate([mm(main, vt, TN), mm(rest, vt, TN)], axis=0)
            dk = dk_in[qk_rows(h), :] + features_back(dphi, x)
            rim_k = rim_ref[qk_rows(h), :].astype(F32)
            rim_v = rim_ref[pl.ds(pl.multiple_of(H * FD + h * DV, DV), DV), :].astype(F32)
            dkt[qk_rows(h), 0:128] = dk[:, :128]
            dkt[qk_rows(h), 128:256] = dk[:, 128:] + rim_k
            dvt[v_rows(h), 0:128] = dv[:, :128].astype(BF16)
            dvt[v_rows(h), 128:256] = (dv[:, 128:] + rim_v).astype(BF16)

    for c in range(H * FD // LANES):
        cols = slice(c * LANES, (c + 1) * LANES)
        kg_ref[:, cols] = dkt[cols, :].T.astype(BF16)
    for c in range(MAIN // LANES):
        cols = slice(c * LANES, (c + 1) * LANES)
        vg_ref[:, cols] = dvt[cols, :].T


def whole(n, rows, q_ref, k_ref, v_ref, do_ref, gain_in, out_ref, qg_ref, kg_ref, vg_ref,
          state, got1, send2, prefix, dstate, got3, send4, suffix, rim_out, rim_in,
          qt, dot, dnum, outt, num, win, dq, dk, dv, dqt, dkt, dvt, kx, vx, ktx, vtx, gain,
          send_sem, recv_sem, rim_send, rim_recv):
    me = lax.axis_index("seq")
    barrier = pltpu.get_barrier_semaphore()

    def peer(step):
        return lax.rem(me + step, n)

    @pl.loop(1, n)
    def _(step):
        pl.semaphore_signal(barrier, inc=1, device_id={"seq": peer(step)}, device_id_type=pl.DeviceIdType.MESH)

    def remote(src, dst, ssem, rsem, to):
        return pltpu.make_async_remote_copy(
            src_ref=src, dst_ref=dst, send_sem=ssem, recv_sem=rsem,
            device_id={"seq": to}, device_id_type=pl.DeviceIdType.MESH)

    def chunk(ref, i):
        return ref.at[pl.ds(pl.multiple_of(i * rows, 16), rows), :]

    def exchange_start(phase, src, dst):
        @pl.loop(1, n)
        def _(step):
            j = peer(step)
            remote(chunk(src, j), chunk(dst, me), send_sem.at[phase, j], recv_sem.at[phase, me], j).start()

        chunk(dst, me)[...] = chunk(src, me)[...]

    def exchange_wait(phase, src, dst):
        @pl.loop(1, n)
        def _(step):
            j = peer(n - step)
            copy = remote(chunk(src, j), chunk(dst, j), send_sem.at[phase, j], recv_sem.at[phase, j], j)
            copy.wait_recv()
            copy.wait_send()

    def scan(src, dst, reverse):
        def step(i, total):
            at = n - 1 - i if reverse else i
            chunk(dst, at)[...] = total.astype(BF16)
            return total + chunk(src, at)[...].astype(F32)

        lax.fori_loop(0, n, step, jnp.zeros((rows, LANES), F32))

    kt = ktx.at[:, 128:384]
    vt = vtx.at[:, 128:384]
    turn(kt, k_ref)
    turn(vt, v_ref)
    if n * rows > PACKED:
        for ref in (state, dstate):
            ref[PACKED:, :] = jnp.zeros((n * rows - PACKED, LANES), BF16)

    @pl.loop(0, H // 4)
    def _(group):
        def one(h, i):
            phi = features(kt[qk_rows(h), :].astype(F32))
            return mm(vt[v_rows(h), :], phi, NT)

        put_state(state, group, heads4(group, one))

    first = me == 0
    end = me == n - 1
    after = jnp.minimum(me + 1, n - 1)
    before = jnp.maximum(me - 1, 0)
    pl.semaphore_wait(barrier, n - 1)

    def rim_copies(to):
        return [
            remote(k_ref.at[BLK - WIN :, :], kx.at[64:128, :], rim_send.at[0], rim_recv.at[0], to),
            remote(v_ref.at[BLK - WIN :, :], vx.at[64:128, :], rim_send.at[1], rim_recv.at[1], to),
        ]

    @pl.when(jnp.logical_not(end))
    def _():
        for copy in rim_copies(after):
            copy.start()

    exchange_start(0, state, got1)
    turn(qt, q_ref)
    turn(dot, do_ref)
    kx[0:64, :] = jnp.zeros((64, H * FD), BF16)
    kx[128:384, :] = k_ref[...]
    vx[0:64, :] = jnp.zeros((64, MAIN), BF16)
    vx[128:384, :] = v_ref[...]
    for c in range(MAIN // LANES):
        gain[c * LANES : (c + 1) * LANES, :] = jnp.broadcast_to(gain_in[c : c + 1, :], (LANES, LANES)).T

    @pl.when(first)
    def _():
        kx[64:128, :] = jnp.zeros((64, H * FD), BF16)
        vx[64:128, :] = jnp.zeros((64, MAIN), BF16)

    @pl.when(jnp.logical_not(first))
    def _():
        for copy in rim_copies(before):
            copy.wait_recv()

    @pl.when(jnp.logical_not(end))
    def _():
        for copy in rim_copies(after):
            copy.wait_send()

    turn(ktx.at[:, 0:128], kx.at[0:128, :])
    turn(vtx.at[:, 0:128], vx.at[0:128, :])
    stage_local(0, first, qt, dot, num, win, dq, dk, dv, kx, vx, ktx, vtx)
    exchange_wait(0, state, got1)
    scan(got1, send2, False)
    exchange_start(1, send2, prefix)
    stage_local(1, first, qt, dot, num, win, dq, dk, dv, kx, vx, ktx, vtx)
    rim_out[0 : H * FD, :] = dk[:, 0:128].astype(BF16)
    rim_out[H * FD :, :] = dv[:, 0:128].astype(BF16)
    exchange_wait(1, send2, prefix)
    stage_mix(prefix, qt, dot, num, win, gain, dnum, dstate, outt)

    def rim_back(to):
        return remote(rim_out, rim_in, rim_send.at[2], rim_recv.at[2], to)

    exchange_start(2, dstate, got3)

    @pl.when(jnp.logical_not(first))
    def _():
        rim_back(before).start()

    turn_out(out_ref, outt)
    dkl = dk.at[:, 128:384]
    dvl = dv.at[:, 128:384]
    stage_back(0, prefix, qt, kt, k_ref, v_ref, dnum, dq, dkl, dvl, dqt)
    exchange_wait(2, dstate, got3)
    scan(got3, send4, True)
    exchange_start(3, send4, suffix)
    stage_back(1, prefix, qt, kt, k_ref, v_ref, dnum, dq, dkl, dvl, dqt)
    turn_out(qg_ref, dqt)

    @pl.when(end)
    def _():
        rim_in[...] = jnp.zeros_like(rim_in)

    @pl.when(jnp.logical_not(end))
    def _():
        rim_back(after).wait_recv()

    @pl.when(jnp.logical_not(first))
    def _():
        rim_back(before).wait_send()

    exchange_wait(3, send4, suffix)
    stage_last(suffix, kt, vt, dkl, dvl, rim_in, kg_ref, vg_ref, dkt, dvt)


def turn_out(dst, src):
    for c in range(dst.shape[1] // LANES):
        cols = slice(c * LANES, (c + 1) * LANES)
        dst[:, cols] = src[cols, :].T.astype(BF16)


def on_device(q, k, v, do, gain):
    n = lax.axis_size("seq")
    rows = -(-PACKED // (16 * n)) * 16
    vm = pltpu.VMEM
    packed = vm((n * rows, LANES), BF16)
    qk, vv = (H * FD, BLK), (MAIN, BLK)
    return pl.pallas_call(
        functools.partial(whole, n, rows),
        out_shape=[jax.ShapeDtypeStruct(x.shape, BF16) for x in (do, q, k, v)],
        in_specs=[pl.BlockSpec(memory_space=vm)] * 5,
        out_specs=[pl.BlockSpec(memory_space=vm)] * 4,
        scratch_shapes=[packed] * 8 + [vm((H * FD + MAIN, LANES), BF16)] * 2 + [
            vm(qk, BF16), vm(vv, BF16), vm(vv, BF16), vm(vv, BF16), vm(vv, F32), vm(vv, F32),
            vm(qk, F32), vm((H * FD, 384), F32), vm((MAIN, 384), F32),
            vm(qk, F32), vm(qk, F32), vm(vv, BF16),
            vm((384, H * FD), BF16), vm((384, MAIN), BF16), vm((H * FD, 384), BF16), vm((MAIN, 384), BF16),
            vm((MAIN, LANES), F32),
            pltpu.SemaphoreType.DMA((4, n)), pltpu.SemaphoreType.DMA((4, n)),
            pltpu.SemaphoreType.DMA((3,)), pltpu.SemaphoreType.DMA((3,)),
        ],
        compiler_params=pltpu.CompilerParams(
            vmem_limit_bytes=56 * 1024 * 1024, collective_id=0, has_side_effects=True),
    )(q, k, v, do, gain.reshape(MAIN // LANES, LANES))


def solution(mesh):
    split = P(("groups", "seq"), None)
    return jax.shard_map(
        on_device, mesh=mesh, in_specs=(split,) * 4 + (P(),), out_specs=(split,) * 4, check_vma=False
    )
```

```python
import functools

import jax
import jax.numpy as jnp
from jax import lax
from jax.experimental import pallas as pl
from jax.experimental.pallas import tpu as pltpu
from jax.sharding import PartitionSpec as P

H = 16
FD = 16
DV = 64
WIN = 64
BLK = 256
LANES = 128
MAIN = H * DV
PACKED = MAIN + MAIN // 4
QUAD = 0.17677669529663687
EPS = 1e-06
NEG = -1e30
F32 = jnp.float32
BF16 = jnp.bfloat16

NN = (((1,), (0,)), ((), ()))
NT = (((1,), (1,)), ((), ()))
TN = (((0,), (0,)), ((), ()))


def mm(a, b, dims=NN):
    return lax.dot_general(a, b, dims, preferred_element_type=F32)


def features(x):
    parts = [x * x * QUAD]
    for d in range(1, 8):
        parts.append(x * pltpu.roll(x, FD - d, 0) * 0.25)
    parts.append(x[:8] * x[8:] * 0.25)
    row = lax.broadcasted_iota(jnp.int32, (8, x.shape[1]), 0)
    parts.append(jnp.where(row == 0, 1.0, 0.0).astype(F32))
    parts.append(x * 0.5)
    return jnp.concatenate(parts, axis=0).astype(BF16)


def features_back(g, x):
    dx = (2.0 * QUAD) * g[:FD] * x
    for d in range(1, 8):
        part = g[d * FD : (d + 1) * FD] * 0.25
        dx = dx + part * pltpu.roll(x, FD - d, 0) + pltpu.roll(part * x, d, 0)
    half = g[128:136] * 0.25
    dx = dx + jnp.concatenate([half * x[8:], half * x[:8]], axis=0)
    return dx + 0.5 * g[144:160]


def turn(dst, src):
    for c in range(src.shape[1] // LANES):
        cols = slice(c * LANES, (c + 1) * LANES)
        dst[cols, :] = src[:, cols].T


def heads4(group, body):
    return [body(group * 4 + i, i) for i in range(4)]


def put_state(buf, group, states):
    for i, st in enumerate(states):
        buf[pl.ds(pl.multiple_of(group * 256 + i * 64, 64), 64), :] = st[:, :128].astype(BF16)
    rest = jnp.concatenate([st[:, 128:160] for st in states], axis=1)
    buf[pl.ds(pl.multiple_of(MAIN + group * 64, 64), 64), :] = rest.astype(BF16)


def get_state(buf, group, i):
    main = buf[pl.ds(pl.multiple_of(group * 256 + i * 64, 64), 64), :]
    rest = buf[pl.ds(pl.multiple_of(MAIN + group * 64, 64), 64), :][:, i * 32 : (i + 1) * 32]
    return main, rest


def qk_rows(h):
    return pl.ds(pl.multiple_of(h * FD, FD), FD)


def v_rows(h):
    return pl.ds(pl.multiple_of(h * DV, DV), DV)


def head_mask(rows, width, which):
    row = lax.broadcasted_iota(jnp.int32, (128, rows), 0)
    return (row >= which * width) & (row < (which + 1) * width)


def tile_scores(kx, q_all, j, head8):
    zero = jnp.zeros_like(q_all)
    picked = jnp.where(head_mask(LANES, FD, head8), q_all, zero)
    return mm(kx, picked) * 0.25


def kernel_mask():
    r = lax.broadcasted_iota(jnp.int32, (128, 128), 0)
    c = lax.broadcasted_iota(jnp.int32, (128, 128), 1)
    return r <= c


def stage_local(half, first, qt_ref, dot_ref, num_ref, win_ref, dq_ref, dk_ref, dv_ref, kx, vx, ktx, vtx):
    lowest = jnp.where(first, 64, 0)
    r = lax.broadcasted_iota(jnp.int32, (192, 128), 0)
    c = lax.broadcasted_iota(jnp.int32, (192, 128), 1)
    band = (r >= c + 1) & (r <= c + 64)
    band0 = band & (r >= lowest)
    below = kernel_mask()
    kcols = slice(half * LANES, (half + 1) * LANES)

    @pl.loop(0, 4)
    def _(pair):
        prow = pl.ds(pl.multiple_of(half * 512 + pair * LANES, LANES), LANES)
        for i in range(2):
            head8 = pair * 2 + i
            h = half * 8 + head8
            dks = []
            dvs = []
            for j in range(2):
                cols = slice(j * 128, (j + 1) * 128)
                keys = slice(j * 128, j * 128 + 256)
                s = tile_scores(kx[keys, kcols], qt_ref[kcols, cols], j, head8)
                kern = 1.0 + s + 0.5 * s * s
                last = jnp.where(below, kern[128:], 0.0).astype(BF16)
                if j == 0:
                    local = mm(vtx[v_rows(h), 128:256], last)
                else:
                    local = mm(vtx[v_rows(h), 128:384],
                               jnp.concatenate([kern[:128].astype(BF16), last], axis=0))
                num_ref[v_rows(h), cols] = local
                sw = jnp.where(band0 if j == 0 else band, s[64:], NEG)
                e = jnp.exp(sw - jnp.max(sw, axis=0, keepdims=True))
                p = e * (1.0 / jnp.sum(e, axis=0, keepdims=True))
                w = p.astype(BF16)
                pad = jnp.zeros((64, 128), BF16)
                wide = jnp.concatenate([pad, w], axis=0)
                win_ref[v_rows(h), cols] = mm(vtx[v_rows(h), keys], wide)
                do_pair = dot_ref[prow, cols]
                do_one = jnp.where(head_mask(LANES, DV, i), do_pair, jnp.zeros_like(do_pair))
                vpair = vx[j * 128 + 64 : j * 128 + 256, pl.ds(pl.multiple_of(half * 512 + pair * LANES, LANES), LANES)]
                dw = mm(vpair, do_one)
                ds = p * (dw - jnp.sum(p * dw, axis=0, keepdims=True)) * 0.25
                ds = jnp.concatenate([pad, ds.astype(BF16)], axis=0)
                dq_ref[qk_rows(h), cols] = mm(ktx[qk_rows(h), keys], ds)
                dks.append(mm(qt_ref[qk_rows(h), cols], ds, NT))
                dvs.append(mm(dot_ref[v_rows(h), cols], wide, NT))
            for dst, rows, parts in ((dk_ref, qk_rows(h), dks), (dv_ref, v_rows(h), dvs)):
                dst[rows, 0:128] = parts[0][:, :128]
                dst[rows, 128:256] = parts[0][:, 128:] + parts[1][:, :128]
                dst[rows, 256:384] = parts[1][:, 128:]


def stage_mix(prefix_ref, qt_ref, dot_ref, num_ref, win_ref, gain_ref,
              dnum_ref, state_ref, outt):
    @pl.loop(0, H // 4)
    def _(group):
        def one(h, i):
            phi = features(qt_ref[qk_rows(h), :].astype(F32))
            main, rest = get_state(prefix_ref, group, i)
            num = num_ref[v_rows(h), :] + mm(main, phi[:128]) + mm(rest, phi[128:])
            inv = lax.rsqrt(jnp.mean(num * num, axis=0, keepdims=True) + EPS)
            gain = jnp.concatenate([gain_ref[v_rows(h), :]] * 2, axis=1)
            unit = num * inv
            outt[v_rows(h), :] = (unit * gain + win_ref[v_rows(h), :]).astype(BF16)
            dg = dot_ref[v_rows(h), :].astype(F32) * gain
            dnum = inv * (dg - unit * jnp.mean(dg * unit, axis=0, keepdims=True))
            half = dnum.astype(BF16)
            dnum_ref[v_rows(h), :] = half
            return mm(half, phi, NT)

        put_state(state_ref, group, heads4(group, one))


def stage_back(half, prefix_ref, qt_ref, kt_ref, k_ref, v_ref, dnum_ref, dq_in, dk_in, dv_in, dqt):
    below = kernel_mask()
    kcols = slice(half * LANES, (half + 1) * LANES)
    dk_ref, dv_ref = dk_in, dv_in

    @pl.loop(0, 2)
    def _(sub):
        group = half * 2 + sub
        for i in range(4):
            head8 = sub * 4 + i
            h = half * 8 + head8
            pcol = pl.ds(pl.multiple_of((group * 2 + i // 2) * LANES, LANES), LANES)
            dk = dk_in[qk_rows(h), :]
            dv = dv_in[v_rows(h), :]
            main, rest = get_state(prefix_ref, group, i)
            dnum = dnum_ref[v_rows(h), :]
            dphi = jnp.concatenate([mm(main, dnum, TN), mm(rest, dnum, TN)], axis=0)
            dq = dq_in[qk_rows(h), :] + features_back(dphi, qt_ref[qk_rows(h), :].astype(F32))
            dqs = []
            for j in range(2):
                cols = slice(j * 128, (j + 1) * 128)
                n = (j + 1) * 128
                s = tile_scores(k_ref[:n, kcols], qt_ref[kcols, cols], j, head8)
                dn_pair = dnum_ref[pcol, cols]
                dn_one = jnp.where(head_mask(LANES, DV, i % 2), dn_pair, jnp.zeros_like(dn_pair))
                dkern = mm(v_ref[:n, pcol], dn_one)
                kern = 1.0 + s + 0.5 * s * s
                ds = dkern * (0.25 + 0.25 * s)
                if j == 0:
                    kern = jnp.where(below, kern, 0.0).astype(BF16)
                    ds = jnp.where(below, ds, 0.0).astype(BF16)
                else:
                    kern = jnp.concatenate(
                        [kern[:128].astype(BF16), jnp.where(below, kern[128:], 0.0).astype(BF16)], axis=0)
                    ds = jnp.concatenate(
                        [ds[:128].astype(BF16), jnp.where(below, ds[128:], 0.0).astype(BF16)], axis=0)
                dqs.append(mm(kt_ref[qk_rows(h), :n], ds))
                dka = mm(qt_ref[qk_rows(h), cols], ds, NT)
                dva = mm(dnum_ref[v_rows(h), cols], kern, NT)
                if j == 0:
                    dka = jnp.concatenate([dka, jnp.zeros_like(dka)], axis=1)
                    dva = jnp.concatenate([dva, jnp.zeros_like(dva)], axis=1)
                dk = dk + dka
                dv = dv + dva
            dqt[qk_rows(h), :] = dq + jnp.concatenate(dqs, axis=1)
            dk_ref[qk_rows(h), :] = dk
            dv_ref[v_rows(h), :] = dv


def stage_last(suffix_ref, kt_ref, vt_ref, dk_in, dv_in, rim_ref, dkt, dvt):
    @pl.loop(0, H // 4)
    def _(group):
        for i in range(4):
            h = group * 4 + i
            main, rest = get_state(suffix_ref, group, i)
            x = kt_ref[qk_rows(h), :].astype(F32)
            phi = features(x)
            vt = vt_ref[v_rows(h), :]
            dv = dv_in[v_rows(h), :] + mm(main, phi[:128]) + mm(rest, phi[128:])
            dphi = jnp.concatenate([mm(main, vt, TN), mm(rest, vt, TN)], axis=0)
            dk = dk_in[qk_rows(h), :] + features_back(dphi, x)
            rim_k = rim_ref[qk_rows(h), :].astype(F32)
            rim_v = rim_ref[pl.ds(pl.multiple_of(H * FD + h * DV, DV), DV), :].astype(F32)
            dkt[qk_rows(h), 0:128] = dk[:, :128].astype(BF16)
            dkt[qk_rows(h), 128:256] = (dk[:, 128:] + rim_k).astype(BF16)
            dvt[v_rows(h), 0:128] = dv[:, :128].astype(BF16)
            dvt[v_rows(h), 128:256] = (dv[:, 128:] + rim_v).astype(BF16)


def whole(n, rows, q_ref, k_ref, v_ref, do_ref, gain_in, out_ref, qg_ref, dkt, dvt,
          state, prefix, dstate, suffix, pair1, sum1, got1, send2, base1, out1,
          pair3, sum3, got3, send4, base3, out3, rim_out, rim_in,
          qt, dot, dnum, outt, num, win, dq, dk, dv, dqt, kx, vx, ktx, vtx, gain,
          send_sem, recv_sem, pair_send, pair_recv, rim_send, rim_recv):
    me = lax.axis_index("seq")
    chips = n // 2
    chip = me // 2
    core = lax.rem(me, 2)
    other_core = 1 - core
    other = chip * 2 + other_core
    barrier = pltpu.get_barrier_semaphore()

    def peer(step):
        return lax.rem(me + step, n)

    @pl.loop(1, n)
    def _(step):
        pl.semaphore_signal(barrier, inc=1, device_id={"seq": peer(step)}, device_id_type=pl.DeviceIdType.MESH)

    def remote(src, dst, ssem, rsem, to):
        return pltpu.make_async_remote_copy(
            src_ref=src, dst_ref=dst, send_sem=ssem, recv_sem=rsem,
            device_id={"seq": to}, device_id_type=pl.DeviceIdType.MESH)

    def chunk(ref, i):
        return ref.at[pl.ds(pl.multiple_of(i * rows, 16), rows), :]

    def half(ref, which):
        return ref.at[pl.ds(pl.multiple_of(which * rows * chips, 16), rows * chips), :]

    def pair_copy(index, src, dst):
        return remote(src, dst, pair_send.at[index], pair_recv.at[index], other)

    def exchange_start(phase, src, dst):
        @pl.loop(1, chips)
        def _(step):
            j = lax.rem(chip + step, chips)
            remote(chunk(src, j), chunk(dst, chip), send_sem.at[phase, j], recv_sem.at[phase, chip], j * 2 + core).start()

        chunk(dst, chip)[...] = chunk(src, chip)[...]

    def exchange_wait(phase, src, dst):
        @pl.loop(1, chips)
        def _(step):
            j = lax.rem(chip + chips - step, chips)
            copy = remote(chunk(src, j), chunk(dst, j), send_sem.at[phase, j], recv_sem.at[phase, j], j * 2 + core)
            copy.wait_recv()
            copy.wait_send()

    def scan(src, dst, reverse):
        def step(i, total):
            at = chips - 1 - i if reverse else i
            chunk(dst, at)[...] = total.astype(BF16)
            return total + chunk(src, at)[...].astype(F32)

        lax.fori_loop(0, chips, step, jnp.zeros((rows, LANES), F32))

    def chip_sum(index, src, got, dst):
        copy = pair_copy(index, half(src, other_core), got)
        copy.wait_recv()
        copy.wait_send()
        dst[...] = (half(src, core)[...].astype(F32) + got[...].astype(F32)).astype(BF16)

    def share(index, base, src, got, out, dst, adds_first):
        sums = base[...].astype(F32)
        mine = half(src, core)[...].astype(F32)
        theirs = got[...].astype(F32)
        i_add = core == adds_first
        zero = jnp.zeros_like(sums)
        out[...] = (sums + jnp.where(i_add, zero, mine)).astype(BF16)
        pair_copy(index, out, half(dst, core)).start()
        half(dst, core)[...] = (sums + jnp.where(i_add, theirs, zero)).astype(BF16)

    def share_wait(index, out, dst):
        copy = pair_copy(index, out, half(dst, other_core))
        copy.wait_recv()
        copy.wait_send()

    kt = ktx.at[:, 128:384]
    vt = vtx.at[:, 128:384]
    turn(kt, k_ref)
    turn(vt, v_ref)
    if n * rows > PACKED:
        for ref in (state, dstate):
            ref[PACKED:, :] = jnp.zeros((n * rows - PACKED, LANES), BF16)

    @pl.loop(0, H // 4)
    def _(group):
        def one(h, i):
            phi = features(kt[qk_rows(h), :].astype(F32))
            return mm(vt[v_rows(h), :], phi, NT)

        put_state(state, group, heads4(group, one))

    first = me == 0
    end = me == n - 1
    after = jnp.minimum(me + 1, n - 1)
    before = jnp.maximum(me - 1, 0)
    pl.semaphore_wait(barrier, n - 1)

    def rim_copies(to):
        return [
            remote(k_ref.at[BLK - WIN :, :], kx.at[64:128, :], rim_send.at[0], rim_recv.at[0], to),
            remote(v_ref.at[BLK - WIN :, :], vx.at[64:128, :], rim_send.at[1], rim_recv.at[1], to),
        ]

    @pl.when(jnp.logical_not(end))
    def _():
        for copy in rim_copies(after):
            copy.start()

    pair_copy(0, half(state, other_core), pair1).start()
    turn(qt, q_ref)
    turn(dot, do_ref)
    kx[0:64, :] = jnp.zeros((64, H * FD), BF16)
    kx[128:384, :] = k_ref[...]
    vx[0:64, :] = jnp.zeros((64, MAIN), BF16)
    vx[128:384, :] = v_ref[...]
    for c in range(MAIN // LANES):
        gain[c * LANES : (c + 1) * LANES, :] = jnp.broadcast_to(gain_in[c : c + 1, :], (LANES, LANES)).T

    @pl.when(first)
    def _():
        kx[64:128, :] = jnp.zeros((64, H * FD), BF16)
        vx[64:128, :] = jnp.zeros((64, MAIN), BF16)

    @pl.when(jnp.logical_not(first))
    def _():
        for copy in rim_copies(before):
            copy.wait_recv()

    @pl.when(jnp.logical_not(end))
    def _():
        for copy in rim_copies(after):
            copy.wait_send()

    chip_sum(0, state, pair1, sum1)
    exchange_start(0, sum1, got1)
    turn(ktx.at[:, 0:128], kx.at[0:128, :])
    turn(vtx.at[:, 0:128], vx.at[0:128, :])
    stage_local(0, first, qt, dot, num, win, dq, dk, dv, kx, vx, ktx, vtx)
    exchange_wait(0, sum1, got1)
    scan(got1, send2, False)
    exchange_start(1, send2, base1)
    stage_local(1, first, qt, dot, num, win, dq, dk, dv, kx, vx, ktx, vtx)
    exchange_wait(1, send2, base1)
    share(1, base1, state, pair1, out1, prefix, 1)
    rim_out[0 : H * FD, :] = dk[:, 0:128].astype(BF16)
    rim_out[H * FD :, :] = dv[:, 0:128].astype(BF16)
    share_wait(1, out1, prefix)
    stage_mix(prefix, qt, dot, num, win, gain, dnum, dstate, outt)

    def rim_back(to):
        return remote(rim_out, rim_in, rim_send.at[2], rim_recv.at[2], to)

    pair_copy(2, half(dstate, other_core), pair3).start()

    @pl.when(jnp.logical_not(first))
    def _():
        rim_back(before).start()

    turn_out(out_ref, outt)
    chip_sum(2, dstate, pair3, sum3)
    exchange_start(2, sum3, got3)
    dkl = dk.at[:, 128:384]
    dvl = dv.at[:, 128:384]
    stage_back(0, prefix, qt, kt, k_ref, v_ref, dnum, dq, dkl, dvl, dqt)
    exchange_wait(2, sum3, got3)
    scan(got3, send4, True)
    exchange_start(3, send4, base3)
    stage_back(1, prefix, qt, kt, k_ref, v_ref, dnum, dq, dkl, dvl, dqt)
    exchange_wait(3, send4, base3)
    share(3, base3, dstate, pair3, out3, suffix, 0)
    turn_out(qg_ref, dqt)

    @pl.when(end)
    def _():
        rim_in[...] = jnp.zeros_like(rim_in)

    @pl.when(jnp.logical_not(end))
    def _():
        rim_back(after).wait_recv()

    @pl.when(jnp.logical_not(first))
    def _():
        rim_back(before).wait_send()

    share_wait(3, out3, suffix)
    stage_last(suffix, kt, vt, dkl, dvl, rim_in, dkt, dvt)


def turn_out(dst, src):
    for c in range(dst.shape[1] // LANES):
        cols = slice(c * LANES, (c + 1) * LANES)
        dst[:, cols] = src[cols, :].T.astype(BF16)


def finish(out_in, qg_in, dkt, dvt, out_ref, qg_ref, kg_ref, vg_ref):
    out_ref[...] = out_in[...]
    qg_ref[...] = qg_in[...]
    turn_out(kg_ref, dkt)
    turn_out(vg_ref, dvt)


def on_device(q, k, v, do, gain):
    n = lax.axis_size("seq")
    rows = -(-PACKED // (16 * n)) * 16
    chips = n // 2
    vm = pltpu.VMEM
    packed = vm((n * rows, LANES), BF16)
    qk, vv = (H * FD, BLK), (MAIN, BLK)
    outs = pl.pallas_call(
        functools.partial(whole, n, rows),
        out_shape=[jax.ShapeDtypeStruct(x.shape, BF16) for x in (do, q)] + [
            jax.ShapeDtypeStruct(s, BF16) for s in (qk, vv)],
        in_specs=[pl.BlockSpec(memory_space=vm)] * 5,
        out_specs=[pl.BlockSpec(memory_space=vm)] * 4,
        scratch_shapes=[packed] * 4 + [vm((chips * rows, LANES), BF16)] * 12 + [vm((H * FD + MAIN, LANES), BF16)] * 2 + [
            vm(qk, BF16), vm(vv, BF16), vm(vv, BF16), vm(vv, BF16), vm(vv, F32), vm(vv, F32),
            vm(qk, F32), vm((H * FD, 384), F32), vm((MAIN, 384), F32),
            vm(qk, F32),
            vm((384, H * FD), BF16), vm((384, MAIN), BF16), vm((H * FD, 384), BF16), vm((MAIN, 384), BF16),
            vm((MAIN, LANES), F32),
            pltpu.SemaphoreType.DMA((4, chips)), pltpu.SemaphoreType.DMA((4, chips)),
            pltpu.SemaphoreType.DMA((4,)), pltpu.SemaphoreType.DMA((4,)),
            pltpu.SemaphoreType.DMA((3,)), pltpu.SemaphoreType.DMA((3,)),
        ],
        compiler_params=pltpu.CompilerParams(
            vmem_limit_bytes=56 * 1024 * 1024, collective_id=0, has_side_effects=True),
    )(q, k, v, do, gain.reshape(MAIN // LANES, LANES))
    steps = 2
    whole_cols = [pl.BlockSpec((BLK, x // steps), lambda i: (0, i)) for x in (MAIN, H * FD, H * FD, MAIN)]
    turned = [pl.BlockSpec((x // steps, BLK), lambda i: (i, 0)) for x in (H * FD, MAIN)]
    return pl.pallas_call(
        finish,
        grid=(steps,),
        out_shape=[jax.ShapeDtypeStruct(x.shape, BF16) for x in (do, q, k, v)],
        in_specs=whole_cols[:2] + turned,
        out_specs=whole_cols,
    )(*outs)


def solution(mesh):
    split = P(("groups", "seq"), None)
    return jax.shard_map(
        on_device, mesh=mesh, in_specs=(split,) * 4 + (P(),), out_specs=(split,) * 4, check_vma=False
    )
```

```python
import functools

import jax
import jax.numpy as jnp
from jax import lax
from jax.experimental import pallas as pl
from jax.experimental.pallas import tpu as pltpu
from jax.sharding import PartitionSpec as P

H = 16
FD = 16
DV = 64
WIN = 64
BLK = 256
LANES = 128
MAIN = H * DV
PACKED = MAIN + MAIN // 4
QUAD = 0.17677669529663687
EPS = 1e-06
NEG = -1e30
F32 = jnp.float32
BF16 = jnp.bfloat16

NN = (((1,), (0,)), ((), ()))
NT = (((1,), (1,)), ((), ()))
TN = (((0,), (0,)), ((), ()))


def mm(a, b, dims=NN):
    return lax.dot_general(a, b, dims, preferred_element_type=F32)


def features(x):
    parts = [x * x * QUAD]
    for d in range(1, 8):
        parts.append(x * pltpu.roll(x, FD - d, 0) * 0.25)
    parts.append(x[:8] * x[8:] * 0.25)
    row = lax.broadcasted_iota(jnp.int32, (8, x.shape[1]), 0)
    parts.append(jnp.where(row == 0, 1.0, 0.0).astype(F32))
    parts.append(x * 0.5)
    return jnp.concatenate(parts, axis=0).astype(BF16)


def features_back(g, x):
    dx = (2.0 * QUAD) * g[:FD] * x
    for d in range(1, 8):
        part = g[d * FD : (d + 1) * FD] * 0.25
        dx = dx + part * pltpu.roll(x, FD - d, 0) + pltpu.roll(part * x, d, 0)
    half = g[128:136] * 0.25
    dx = dx + jnp.concatenate([half * x[8:], half * x[:8]], axis=0)
    return dx + 0.5 * g[144:160]


def turn(dst, src):
    for c in range(src.shape[1] // LANES):
        cols = slice(c * LANES, (c + 1) * LANES)
        dst[cols, :] = src[:, cols].T


def heads4(group, body):
    return [body(group * 4 + i, i) for i in range(4)]


def put_state(buf, group, states):
    for i, st in enumerate(states):
        buf[pl.ds(pl.multiple_of(group * 256 + i * 64, 64), 64), :] = st[:, :128].astype(BF16)
    rest = jnp.concatenate([st[:, 128:160] for st in states], axis=1)
    buf[pl.ds(pl.multiple_of(MAIN + group * 64, 64), 64), :] = rest.astype(BF16)


def get_state(buf, group, i):
    main = buf[pl.ds(pl.multiple_of(group * 256 + i * 64, 64), 64), :]
    rest = buf[pl.ds(pl.multiple_of(MAIN + group * 64, 64), 64), :][:, i * 32 : (i + 1) * 32]
    return main, rest


def qk_rows(h):
    return pl.ds(pl.multiple_of(h * FD, FD), FD)


def v_rows(h):
    return pl.ds(pl.multiple_of(h * DV, DV), DV)


def head_mask(rows, width, which):
    row = lax.broadcasted_iota(jnp.int32, (128, rows), 0)
    return (row >= which * width) & (row < (which + 1) * width)


def tile_scores(kx, q_all, j, head8):
    zero = jnp.zeros_like(q_all)
    picked = jnp.where(head_mask(LANES, FD, head8), q_all, zero)
    return mm(kx, picked) * 0.25


def kernel_mask():
    r = lax.broadcasted_iota(jnp.int32, (128, 128), 0)
    c = lax.broadcasted_iota(jnp.int32, (128, 128), 1)
    return r <= c


def stage_local(half, first, qt_ref, dot_ref, num_ref, win_ref, dq_ref, dk_ref, dv_ref, kx, vx, ktx, vtx):
    lowest = jnp.where(first, 64, 0)
    r = lax.broadcasted_iota(jnp.int32, (192, 128), 0)
    c = lax.broadcasted_iota(jnp.int32, (192, 128), 1)
    band = (r >= c + 1) & (r <= c + 64)
    band0 = band & (r >= lowest)
    below = kernel_mask()
    kcols = slice(half * LANES, (half + 1) * LANES)

    @pl.loop(0, 4)
    def _(pair):
        prow = pl.ds(pl.multiple_of(half * 512 + pair * LANES, LANES), LANES)
        for i in range(2):
            head8 = pair * 2 + i
            h = half * 8 + head8
            dks = []
            dvs = []
            for j in range(2):
                cols = slice(j * 128, (j + 1) * 128)
                keys = slice(j * 128, j * 128 + 256)
                s = tile_scores(kx[keys, kcols], qt_ref[kcols, cols], j, head8)
                kern = 1.0 + s + 0.5 * s * s
                last = jnp.where(below, kern[128:], 0.0).astype(BF16)
                if j == 0:
                    local = mm(vtx[v_rows(h), 128:256], last)
                else:
                    local = mm(vtx[v_rows(h), 128:384],
                               jnp.concatenate([kern[:128].astype(BF16), last], axis=0))
                num_ref[v_rows(h), cols] = local
                sw = jnp.where(band0 if j == 0 else band, s[64:], NEG)
                e = jnp.exp(sw - jnp.max(sw, axis=0, keepdims=True))
                p = e * (1.0 / jnp.sum(e, axis=0, keepdims=True))
                w = p.astype(BF16)
                pad = jnp.zeros((64, 128), BF16)
                wide = jnp.concatenate([pad, w], axis=0)
                win_ref[v_rows(h), cols] = mm(vtx[v_rows(h), keys], wide)
                do_pair = dot_ref[prow, cols]
                do_one = jnp.where(head_mask(LANES, DV, i), do_pair, jnp.zeros_like(do_pair))
                vpair = vx[j * 128 + 64 : j * 128 + 256, pl.ds(pl.multiple_of(half * 512 + pair * LANES, LANES), LANES)]
                dw = mm(vpair, do_one)
                ds = p * (dw - jnp.sum(p * dw, axis=0, keepdims=True)) * 0.25
                ds = jnp.concatenate([pad, ds.astype(BF16)], axis=0)
                dq_ref[qk_rows(h), cols] = mm(ktx[qk_rows(h), keys], ds)
                dks.append(mm(qt_ref[qk_rows(h), cols], ds, NT))
                dvs.append(mm(dot_ref[v_rows(h), cols], wide, NT))
            for dst, rows, parts in ((dk_ref, qk_rows(h), dks), (dv_ref, v_rows(h), dvs)):
                dst[rows, 0:128] = parts[0][:, :128]
                dst[rows, 128:256] = parts[0][:, 128:] + parts[1][:, :128]
                dst[rows, 256:384] = parts[1][:, 128:]


def stage_mix(prefix_ref, qt_ref, dot_ref, num_ref, win_ref, gain_ref,
              dnum_ref, state_ref, outt):
    @pl.loop(0, H // 4, unroll=True)
    def _(group):
        def one(h, i):
            phi = features(qt_ref[qk_rows(h), :].astype(F32))
            main, rest = get_state(prefix_ref, group, i)
            num = num_ref[v_rows(h), :] + mm(main, phi[:128]) + mm(rest, phi[128:])
            inv = lax.rsqrt(jnp.mean(num * num, axis=0, keepdims=True) + EPS)
            gain = jnp.concatenate([gain_ref[v_rows(h), :]] * 2, axis=1)
            unit = num * inv
            outt[v_rows(h), :] = (unit * gain + win_ref[v_rows(h), :]).astype(BF16)
            dg = dot_ref[v_rows(h), :].astype(F32) * gain
            dnum = inv * (dg - unit * jnp.mean(dg * unit, axis=0, keepdims=True))
            half = dnum.astype(BF16)
            dnum_ref[v_rows(h), :] = half
            return mm(half, phi, NT)

        put_state(state_ref, group, heads4(group, one))


def stage_back(half, prefix_ref, qt_ref, kt_ref, k_ref, v_ref, dnum_ref, dq_in, dk_in, dv_in, dqt):
    below = kernel_mask()
    kcols = slice(half * LANES, (half + 1) * LANES)
    dk_ref, dv_ref = dk_in, dv_in

    @pl.loop(0, 2)
    def _(sub):
        group = half * 2 + sub
        for i in range(4):
            head8 = sub * 4 + i
            h = half * 8 + head8
            pcol = pl.ds(pl.multiple_of((group * 2 + i // 2) * LANES, LANES), LANES)
            dk = dk_in[qk_rows(h), :]
            dv = dv_in[v_rows(h), :]
            main, rest = get_state(prefix_ref, group, i)
            dnum = dnum_ref[v_rows(h), :]
            dphi = jnp.concatenate([mm(main, dnum, TN), mm(rest, dnum, TN)], axis=0)
            dq = dq_in[qk_rows(h), :] + features_back(dphi, qt_ref[qk_rows(h), :].astype(F32))
            dqs = []
            for j in range(2):
                cols = slice(j * 128, (j + 1) * 128)
                n = (j + 1) * 128
                s = tile_scores(k_ref[:n, kcols], qt_ref[kcols, cols], j, head8)
                dn_pair = dnum_ref[pcol, cols]
                dn_one = jnp.where(head_mask(LANES, DV, i % 2), dn_pair, jnp.zeros_like(dn_pair))
                dkern = mm(v_ref[:n, pcol], dn_one)
                kern = 1.0 + s + 0.5 * s * s
                ds = dkern * (0.25 + 0.25 * s)
                if j == 0:
                    kern = jnp.where(below, kern, 0.0).astype(BF16)
                    ds = jnp.where(below, ds, 0.0).astype(BF16)
                else:
                    kern = jnp.concatenate(
                        [kern[:128].astype(BF16), jnp.where(below, kern[128:], 0.0).astype(BF16)], axis=0)
                    ds = jnp.concatenate(
                        [ds[:128].astype(BF16), jnp.where(below, ds[128:], 0.0).astype(BF16)], axis=0)
                dqs.append(mm(kt_ref[qk_rows(h), :n], ds))
                dka = mm(qt_ref[qk_rows(h), cols], ds, NT)
                dva = mm(dnum_ref[v_rows(h), cols], kern, NT)
                if j == 0:
                    dka = jnp.concatenate([dka, jnp.zeros_like(dka)], axis=1)
                    dva = jnp.concatenate([dva, jnp.zeros_like(dva)], axis=1)
                dk = dk + dka
                dv = dv + dva
            dqt[qk_rows(h), :] = dq + jnp.concatenate(dqs, axis=1)
            dk_ref[qk_rows(h), :] = dk
            dv_ref[v_rows(h), :] = dv


def stage_last(suffix_ref, kt_ref, vt_ref, dk_in, dv_in, rim_ref, dkt, dvt):
    @pl.loop(0, H // 4, unroll=True)
    def _(group):
        for i in range(4):
            h = group * 4 + i
            main, rest = get_state(suffix_ref, group, i)
            x = kt_ref[qk_rows(h), :].astype(F32)
            phi = features(x)
            vt = vt_ref[v_rows(h), :]
            dv = dv_in[v_rows(h), :] + mm(main, phi[:128]) + mm(rest, phi[128:])
            dphi = jnp.concatenate([mm(main, vt, TN), mm(rest, vt, TN)], axis=0)
            dk = dk_in[qk_rows(h), :] + features_back(dphi, x)
            rim_k = rim_ref[qk_rows(h), :].astype(F32)
            rim_v = rim_ref[pl.ds(pl.multiple_of(H * FD + h * DV, DV), DV), :].astype(F32)
            dkt[qk_rows(h), 0:128] = dk[:, :128].astype(BF16)
            dkt[qk_rows(h), 128:256] = (dk[:, 128:] + rim_k).astype(BF16)
            dvt[v_rows(h), 0:128] = dv[:, :128].astype(BF16)
            dvt[v_rows(h), 128:256] = (dv[:, 128:] + rim_v).astype(BF16)


def whole(n, rows, q_ref, k_ref, v_ref, do_ref, gain_in, out_ref, qg_ref, dkt, dvt,
          state, prefix, dstate, suffix, pair1, sum1, got1, send2, base1, out1,
          pair3, sum3, got3, send4, base3, out3, rim_out, rim_in,
          qt, dot, dnum, outt, num, win, dq, dk, dv, dqt, kx, vx, ktx, vtx, gain,
          send_sem, recv_sem, pair_send, pair_recv, rim_send, rim_recv):
    me = lax.axis_index("seq")
    chips = n // 2
    chip = me // 2
    core = lax.rem(me, 2)
    other_core = 1 - core
    other = chip * 2 + other_core
    barrier = pltpu.get_barrier_semaphore()

    def peer(step):
        return lax.rem(me + step, n)

    @pl.loop(1, n)
    def _(step):
        pl.semaphore_signal(barrier, inc=1, device_id={"seq": peer(step)}, device_id_type=pl.DeviceIdType.MESH)

    def remote(src, dst, ssem, rsem, to):
        return pltpu.make_async_remote_copy(
            src_ref=src, dst_ref=dst, send_sem=ssem, recv_sem=rsem,
            device_id={"seq": to}, device_id_type=pl.DeviceIdType.MESH)

    def chunk(ref, i):
        return ref.at[pl.ds(pl.multiple_of(i * rows, 16), rows), :]

    def half(ref, which):
        return ref.at[pl.ds(pl.multiple_of(which * rows * chips, 16), rows * chips), :]

    def pair_copy(index, src, dst):
        return remote(src, dst, pair_send.at[index], pair_recv.at[index], other)

    def exchange_start(phase, src, dst):
        @pl.loop(1, chips)
        def _(step):
            j = lax.rem(chip + step, chips)
            remote(chunk(src, j), chunk(dst, chip), send_sem.at[phase, j], recv_sem.at[phase, chip], j * 2 + core).start()

        chunk(dst, chip)[...] = chunk(src, chip)[...]

    def exchange_wait(phase, src, dst):
        @pl.loop(1, chips)
        def _(step):
            j = lax.rem(chip + chips - step, chips)
            copy = remote(chunk(src, j), chunk(dst, j), send_sem.at[phase, j], recv_sem.at[phase, j], j * 2 + core)
            copy.wait_recv()
            copy.wait_send()

    def scan(src, dst, reverse):
        def step(i, total):
            at = chips - 1 - i if reverse else i
            chunk(dst, at)[...] = total.astype(BF16)
            return total + chunk(src, at)[...].astype(F32)

        lax.fori_loop(0, chips, step, jnp.zeros((rows, LANES), F32))

    def chip_sum(index, src, got, dst):
        copy = pair_copy(index, half(src, other_core), got)
        copy.wait_recv()
        copy.wait_send()
        dst[...] = (half(src, core)[...].astype(F32) + got[...].astype(F32)).astype(BF16)

    def share(index, base, src, got, out, dst, adds_first):
        sums = base[...].astype(F32)
        mine = half(src, core)[...].astype(F32)
        theirs = got[...].astype(F32)
        i_add = core == adds_first
        zero = jnp.zeros_like(sums)
        out[...] = (sums + jnp.where(i_add, zero, mine)).astype(BF16)
        pair_copy(index, out, half(dst, core)).start()
        half(dst, core)[...] = (sums + jnp.where(i_add, theirs, zero)).astype(BF16)

    def share_wait(index, out, dst):
        copy = pair_copy(index, out, half(dst, other_core))
        copy.wait_recv()
        copy.wait_send()

    kt = ktx.at[:, 128:384]
    vt = vtx.at[:, 128:384]
    turn(kt, k_ref)
    turn(vt, v_ref)
    if n * rows > PACKED:
        for ref in (state, dstate):
            ref[PACKED:, :] = jnp.zeros((n * rows - PACKED, LANES), BF16)

    @pl.loop(0, H // 4, unroll=True)
    def _(group):
        def one(h, i):
            phi = features(kt[qk_rows(h), :].astype(F32))
            return mm(vt[v_rows(h), :], phi, NT)

        put_state(state, group, heads4(group, one))

    first = me == 0
    end = me == n - 1
    after = jnp.minimum(me + 1, n - 1)
    before = jnp.maximum(me - 1, 0)
    pl.semaphore_wait(barrier, n - 1)

    def rim_copies(to):
        return [
            remote(k_ref.at[BLK - WIN :, :], kx.at[64:128, :], rim_send.at[0], rim_recv.at[0], to),
            remote(v_ref.at[BLK - WIN :, :], vx.at[64:128, :], rim_send.at[1], rim_recv.at[1], to),
        ]

    @pl.when(jnp.logical_not(end))
    def _():
        for copy in rim_copies(after):
            copy.start()

    pair_copy(0, half(state, other_core), pair1).start()
    turn(qt, q_ref)
    turn(dot, do_ref)
    chip_sum(0, state, pair1, sum1)
    exchange_start(0, sum1, got1)
    kx[0:64, :] = jnp.zeros((64, H * FD), BF16)
    kx[128:384, :] = k_ref[...]
    vx[0:64, :] = jnp.zeros((64, MAIN), BF16)
    vx[128:384, :] = v_ref[...]
    for c in range(MAIN // LANES):
        gain[c * LANES : (c + 1) * LANES, :] = jnp.broadcast_to(gain_in[c : c + 1, :], (LANES, LANES)).T

    @pl.when(first)
    def _():
        kx[64:128, :] = jnp.zeros((64, H * FD), BF16)
        vx[64:128, :] = jnp.zeros((64, MAIN), BF16)

    @pl.when(jnp.logical_not(first))
    def _():
        for copy in rim_copies(before):
            copy.wait_recv()

    @pl.when(jnp.logical_not(end))
    def _():
        for copy in rim_copies(after):
            copy.wait_send()

    turn(ktx.at[:, 0:128], kx.at[0:128, :])
    turn(vtx.at[:, 0:128], vx.at[0:128, :])
    stage_local(0, first, qt, dot, num, win, dq, dk, dv, kx, vx, ktx, vtx)
    exchange_wait(0, sum1, got1)
    scan(got1, send2, False)
    exchange_start(1, send2, base1)
    stage_local(1, first, qt, dot, num, win, dq, dk, dv, kx, vx, ktx, vtx)
    exchange_wait(1, send2, base1)
    share(1, base1, state, pair1, out1, prefix, 1)
    rim_out[0 : H * FD, :] = dk[:, 0:128].astype(BF16)
    rim_out[H * FD :, :] = dv[:, 0:128].astype(BF16)
    def rim_back(to):
        return remote(rim_out, rim_in, rim_send.at[2], rim_recv.at[2], to)

    @pl.when(jnp.logical_not(first))
    def _():
        rim_back(before).start()

    share_wait(1, out1, prefix)
    stage_mix(prefix, qt, dot, num, win, gain, dnum, dstate, outt)

    pair_copy(2, half(dstate, other_core), pair3).start()

    turn_out(out_ref, outt)
    chip_sum(2, dstate, pair3, sum3)
    exchange_start(2, sum3, got3)
    dkl = dk.at[:, 128:384]
    dvl = dv.at[:, 128:384]
    stage_back(0, prefix, qt, kt, k_ref, v_ref, dnum, dq, dkl, dvl, dqt)
    exchange_wait(2, sum3, got3)
    scan(got3, send4, True)
    exchange_start(3, send4, base3)
    stage_back(1, prefix, qt, kt, k_ref, v_ref, dnum, dq, dkl, dvl, dqt)
    exchange_wait(3, send4, base3)
    share(3, base3, dstate, pair3, out3, suffix, 0)
    turn_out(qg_ref, dqt)

    @pl.when(end)
    def _():
        rim_in[...] = jnp.zeros_like(rim_in)

    @pl.when(jnp.logical_not(end))
    def _():
        rim_back(after).wait_recv()

    @pl.when(jnp.logical_not(first))
    def _():
        rim_back(before).wait_send()

    share_wait(3, out3, suffix)
    stage_last(suffix, kt, vt, dkl, dvl, rim_in, dkt, dvt)


def turn_out(dst, src):
    for c in range(dst.shape[1] // LANES):
        cols = slice(c * LANES, (c + 1) * LANES)
        dst[:, cols] = src[cols, :].T.astype(BF16)


def finish(out_in, qg_in, dkt, dvt, out_ref, qg_ref, kg_ref, vg_ref):
    out_ref[...] = out_in[...]
    qg_ref[...] = qg_in[...]
    turn_out(kg_ref, dkt)
    turn_out(vg_ref, dvt)


def on_device(q, k, v, do, gain):
    n = lax.axis_size("seq")
    rows = -(-PACKED // (16 * n)) * 16
    chips = n // 2
    vm = pltpu.VMEM
    packed = vm((n * rows, LANES), BF16)
    qk, vv = (H * FD, BLK), (MAIN, BLK)
    outs = pl.pallas_call(
        functools.partial(whole, n, rows),
        out_shape=[jax.ShapeDtypeStruct(x.shape, BF16) for x in (do, q)] + [
            jax.ShapeDtypeStruct(s, BF16) for s in (qk, vv)],
        in_specs=[pl.BlockSpec(memory_space=vm)] * 5,
        out_specs=[pl.BlockSpec(memory_space=vm)] * 4,
        scratch_shapes=[packed] * 4 + [vm((chips * rows, LANES), BF16)] * 12 + [vm((H * FD + MAIN, LANES), BF16)] * 2 + [
            vm(qk, BF16), vm(vv, BF16), vm(vv, BF16), vm(vv, BF16), vm(vv, F32), vm(vv, F32),
            vm(qk, F32), vm((H * FD, 384), F32), vm((MAIN, 384), F32),
            vm(qk, F32),
            vm((384, H * FD), BF16), vm((384, MAIN), BF16), vm((H * FD, 384), BF16), vm((MAIN, 384), BF16),
            vm((MAIN, LANES), F32),
            pltpu.SemaphoreType.DMA((4, chips)), pltpu.SemaphoreType.DMA((4, chips)),
            pltpu.SemaphoreType.DMA((4,)), pltpu.SemaphoreType.DMA((4,)),
            pltpu.SemaphoreType.DMA((3,)), pltpu.SemaphoreType.DMA((3,)),
        ],
        compiler_params=pltpu.CompilerParams(
            vmem_limit_bytes=56 * 1024 * 1024, collective_id=0, has_side_effects=True),
    )(q, k, v, do, gain.reshape(MAIN // LANES, LANES))
    steps = 2
    whole_cols = [pl.BlockSpec((BLK, x // steps), lambda i: (0, i)) for x in (MAIN, H * FD, H * FD, MAIN)]
    turned = [pl.BlockSpec((x // steps, BLK), lambda i: (i, 0)) for x in (H * FD, MAIN)]
    return pl.pallas_call(
        finish,
        grid=(steps,),
        out_shape=[jax.ShapeDtypeStruct(x.shape, BF16) for x in (do, q, k, v)],
        in_specs=whole_cols[:2] + turned,
        out_specs=whole_cols,
    )(*outs)


def solution(mesh):
    split = P(("groups", "seq"), None)
    return jax.shard_map(
        on_device, mesh=mesh, in_specs=(split,) * 4 + (P(),), out_specs=(split,) * 4, check_vma=False
    )
```

```python
import functools

import jax
import jax.numpy as jnp
from jax import lax
from jax.experimental import pallas as pl
from jax.experimental.pallas import tpu as pltpu
from jax.sharding import PartitionSpec as P

H = 16
FD = 16
DV = 64
WIN = 64
BLK = 256
LANES = 128
MAIN = H * DV
PACKED = MAIN + MAIN // 4
QUAD = 0.17677669529663687
EPS = 1e-06
NEG = -1e30
F32 = jnp.float32
BF16 = jnp.bfloat16

NN = (((1,), (0,)), ((), ()))
NT = (((1,), (1,)), ((), ()))
TN = (((0,), (0,)), ((), ()))


def mm(a, b, dims=NN):
    return lax.dot_general(a, b, dims, preferred_element_type=F32)


def features(x):
    parts = [x * x * QUAD]
    for d in range(1, 8):
        parts.append(x * pltpu.roll(x, FD - d, 0) * 0.25)
    parts.append(x[:8] * x[8:] * 0.25)
    row = lax.broadcasted_iota(jnp.int32, (8, x.shape[1]), 0)
    parts.append(jnp.where(row == 0, 1.0, 0.0).astype(F32))
    parts.append(x * 0.5)
    return jnp.concatenate(parts, axis=0).astype(BF16)


def features_back(g, x):
    dx = (2.0 * QUAD) * g[:FD] * x
    for d in range(1, 8):
        part = g[d * FD : (d + 1) * FD] * 0.25
        dx = dx + part * pltpu.roll(x, FD - d, 0) + pltpu.roll(part * x, d, 0)
    half = g[128:136] * 0.25
    dx = dx + jnp.concatenate([half * x[8:], half * x[:8]], axis=0)
    return dx + 0.5 * g[144:160]


def turn(dst, src):
    for c in range(src.shape[1] // LANES):
        cols = slice(c * LANES, (c + 1) * LANES)
        dst[cols, :] = src[:, cols].T


def heads4(group, body):
    return [body(group * 4 + i, i) for i in range(4)]


def put_state(buf, group, states):
    for i, st in enumerate(states):
        buf[pl.ds(pl.multiple_of(group * 256 + i * 64, 64), 64), :] = st[:, :128].astype(BF16)
    rest = jnp.concatenate([st[:, 128:160] for st in states], axis=1)
    buf[pl.ds(pl.multiple_of(MAIN + group * 64, 64), 64), :] = rest.astype(BF16)


def get_state(buf, group, i):
    main = buf[pl.ds(pl.multiple_of(group * 256 + i * 64, 64), 64), :]
    rest = buf[pl.ds(pl.multiple_of(MAIN + group * 64, 64), 64), :][:, i * 32 : (i + 1) * 32]
    return main, rest


def qk_rows(h):
    return pl.ds(pl.multiple_of(h * FD, FD), FD)


def v_rows(h):
    return pl.ds(pl.multiple_of(h * DV, DV), DV)


def head_mask(rows, width, which):
    row = lax.broadcasted_iota(jnp.int32, (128, rows), 0)
    return (row >= which * width) & (row < (which + 1) * width)


def tile_scores(kx, q_all, j, head8):
    zero = jnp.zeros_like(q_all)
    picked = jnp.where(head_mask(LANES, FD, head8), q_all, zero)
    return mm(kx, picked) * 0.25


def kernel_mask():
    r = lax.broadcasted_iota(jnp.int32, (128, 128), 0)
    c = lax.broadcasted_iota(jnp.int32, (128, 128), 1)
    return r <= c


def stage_local(half, first, qt_ref, dot_ref, num_ref, win_ref, dq_ref, dk_ref, dv_ref, kx, vx, ktx, vtx):
    lowest = jnp.where(first, 64, 0)
    r = lax.broadcasted_iota(jnp.int32, (192, 128), 0)
    c = lax.broadcasted_iota(jnp.int32, (192, 128), 1)
    band = (r >= c + 1) & (r <= c + 64)
    band0 = band & (r >= lowest)
    below = kernel_mask()
    kcols = slice(half * LANES, (half + 1) * LANES)

    @pl.loop(0, 4)
    def _(pair):
        prow = pl.ds(pl.multiple_of(half * 512 + pair * LANES, LANES), LANES)
        for i in range(2):
            head8 = pair * 2 + i
            h = half * 8 + head8
            dks = []
            dvs = []
            for j in range(2):
                cols = slice(j * 128, (j + 1) * 128)
                keys = slice(j * 128, j * 128 + 256)
                s = tile_scores(kx[keys, kcols], qt_ref[kcols, cols], j, head8)
                kern = 1.0 + s + 0.5 * s * s
                last = jnp.where(below, kern[128:], 0.0).astype(BF16)
                if j == 0:
                    local = mm(vtx[v_rows(h), 128:256], last)
                else:
                    local = mm(vtx[v_rows(h), 128:384],
                               jnp.concatenate([kern[:128].astype(BF16), last], axis=0))
                num_ref[v_rows(h), cols] = local
                sw = jnp.where(band0 if j == 0 else band, s[64:], NEG)
                e = jnp.exp(sw - jnp.max(sw, axis=0, keepdims=True))
                p = e * (1.0 / jnp.sum(e, axis=0, keepdims=True))
                w = p.astype(BF16)
                pad = jnp.zeros((64, 128), BF16)
                wide = jnp.concatenate([pad, w], axis=0)
                win_ref[v_rows(h), cols] = mm(vtx[v_rows(h), keys], wide)
                do_pair = dot_ref[prow, cols]
                do_one = jnp.where(head_mask(LANES, DV, i), do_pair, jnp.zeros_like(do_pair))
                vpair = vx[j * 128 + 64 : j * 128 + 256, pl.ds(pl.multiple_of(half * 512 + pair * LANES, LANES), LANES)]
                dw = mm(vpair, do_one)
                ds = p * (dw - jnp.sum(p * dw, axis=0, keepdims=True)) * 0.25
                ds = jnp.concatenate([pad, ds.astype(BF16)], axis=0)
                dq_ref[qk_rows(h), cols] = mm(ktx[qk_rows(h), keys], ds)
                dks.append(mm(qt_ref[qk_rows(h), cols], ds, NT))
                dvs.append(mm(dot_ref[v_rows(h), cols], wide, NT))
            for dst, rows, parts in ((dk_ref, qk_rows(h), dks), (dv_ref, v_rows(h), dvs)):
                dst[rows, 0:128] = parts[0][:, :128]
                dst[rows, 128:256] = parts[0][:, 128:] + parts[1][:, :128]
                dst[rows, 256:384] = parts[1][:, 128:]


def stage_mix(prefix_ref, qt_ref, dot_ref, num_ref, win_ref, gain_ref,
              dnum_ref, state_ref, outt):
    @pl.loop(0, H // 4, unroll=True)
    def _(group):
        def one(h, i):
            phi = features(qt_ref[qk_rows(h), :].astype(F32))
            main, rest = get_state(prefix_ref, group, i)
            num = num_ref[v_rows(h), :] + mm(main, phi[:128]) + mm(rest, phi[128:])
            inv = lax.rsqrt(jnp.mean(num * num, axis=0, keepdims=True) + EPS)
            gain = jnp.concatenate([gain_ref[v_rows(h), :]] * 2, axis=1)
            unit = num * inv
            outt[v_rows(h), :] = (unit * gain + win_ref[v_rows(h), :]).astype(BF16)
            dg = dot_ref[v_rows(h), :].astype(F32) * gain
            dnum = inv * (dg - unit * jnp.mean(dg * unit, axis=0, keepdims=True))
            half = dnum.astype(BF16)
            dnum_ref[v_rows(h), :] = half
            return mm(half, phi, NT)

        put_state(state_ref, group, heads4(group, one))


def stage_back(half, prefix_ref, qt_ref, kt_ref, k_ref, v_ref, dnum_ref, dq_in, dk_in, dv_in, dqt):
    below = kernel_mask()
    kcols = slice(half * LANES, (half + 1) * LANES)
    dk_ref, dv_ref = dk_in, dv_in

    @pl.loop(0, 2)
    def _(sub):
        group = half * 2 + sub
        for i in range(4):
            head8 = sub * 4 + i
            h = half * 8 + head8
            pcol = pl.ds(pl.multiple_of((group * 2 + i // 2) * LANES, LANES), LANES)
            dk = dk_in[qk_rows(h), :]
            dv = dv_in[v_rows(h), :]
            main, rest = get_state(prefix_ref, group, i)
            dnum = dnum_ref[v_rows(h), :]
            dphi = jnp.concatenate([mm(main, dnum, TN), mm(rest, dnum, TN)], axis=0)
            dq = dq_in[qk_rows(h), :] + features_back(dphi, qt_ref[qk_rows(h), :].astype(F32))
            dqs = []
            for j in range(2):
                cols = slice(j * 128, (j + 1) * 128)
                n = (j + 1) * 128
                s = tile_scores(k_ref[:n, kcols], qt_ref[kcols, cols], j, head8)
                dn_pair = dnum_ref[pcol, cols]
                dn_one = jnp.where(head_mask(LANES, DV, i % 2), dn_pair, jnp.zeros_like(dn_pair))
                dkern = mm(v_ref[:n, pcol], dn_one)
                kern = 1.0 + s + 0.5 * s * s
                ds = dkern * (0.25 + 0.25 * s)
                if j == 0:
                    kern = jnp.where(below, kern, 0.0).astype(BF16)
                    ds = jnp.where(below, ds, 0.0).astype(BF16)
                else:
                    kern = jnp.concatenate(
                        [kern[:128].astype(BF16), jnp.where(below, kern[128:], 0.0).astype(BF16)], axis=0)
                    ds = jnp.concatenate(
                        [ds[:128].astype(BF16), jnp.where(below, ds[128:], 0.0).astype(BF16)], axis=0)
                dqs.append(mm(kt_ref[qk_rows(h), :n], ds))
                dka = mm(qt_ref[qk_rows(h), cols], ds, NT)
                dva = mm(dnum_ref[v_rows(h), cols], kern, NT)
                if j == 0:
                    dka = jnp.concatenate([dka, jnp.zeros_like(dka)], axis=1)
                    dva = jnp.concatenate([dva, jnp.zeros_like(dva)], axis=1)
                dk = dk + dka
                dv = dv + dva
            dqt[qk_rows(h), :] = dq + jnp.concatenate(dqs, axis=1)
            dk_ref[qk_rows(h), :] = dk
            dv_ref[v_rows(h), :] = dv


def stage_last(suffix_ref, kt_ref, vt_ref, dk_in, dv_in, rim_ref, dkt, dvt):
    @pl.loop(0, H // 4, unroll=True)
    def _(group):
        for i in range(4):
            h = group * 4 + i
            main, rest = get_state(suffix_ref, group, i)
            x = kt_ref[qk_rows(h), :].astype(F32)
            phi = features(x)
            vt = vt_ref[v_rows(h), :]
            dv = dv_in[v_rows(h), :] + mm(main, phi[:128]) + mm(rest, phi[128:])
            dphi = jnp.concatenate([mm(main, vt, TN), mm(rest, vt, TN)], axis=0)
            dk = dk_in[qk_rows(h), :] + features_back(dphi, x)
            rim_k = rim_ref[qk_rows(h), :].astype(F32)
            rim_v = rim_ref[pl.ds(pl.multiple_of(H * FD + h * DV, DV), DV), :].astype(F32)
            dkt[qk_rows(h), 0:128] = dk[:, :128].astype(BF16)
            dkt[qk_rows(h), 128:256] = (dk[:, 128:] + rim_k).astype(BF16)
            dvt[v_rows(h), 0:128] = dv[:, :128].astype(BF16)
            dvt[v_rows(h), 128:256] = (dv[:, 128:] + rim_v).astype(BF16)


def whole(n, rows, q_ref, k_ref, v_ref, do_ref, gain_in, out_ref, qg_ref, dkt, dvt,
          state, prefix, dstate, suffix, pair1, sum1, got1, send2, base1, out1,
          pair3, sum3, got3, send4, base3, out3, rim_out, rim_in,
          qt, dot, dnum, outt, num, win, dq, dk, dv, dqt, kx, vx, ktx, vtx, gain,
          send_sem, recv_sem, pair_send, pair_recv, rim_send, rim_recv):
    me = lax.axis_index("seq")
    chips = n // 2
    chip = me // 2
    core = lax.rem(me, 2)
    other_core = 1 - core
    other = chip * 2 + other_core
    barrier = pltpu.get_barrier_semaphore()

    def peer(step):
        return lax.rem(me + step, n)

    @pl.loop(1, n)
    def _(step):
        pl.semaphore_signal(barrier, inc=1, device_id={"seq": peer(step)}, device_id_type=pl.DeviceIdType.MESH)

    def remote(src, dst, ssem, rsem, to):
        return pltpu.make_async_remote_copy(
            src_ref=src, dst_ref=dst, send_sem=ssem, recv_sem=rsem,
            device_id={"seq": to}, device_id_type=pl.DeviceIdType.MESH)

    def chunk(ref, i):
        return ref.at[pl.ds(pl.multiple_of(i * rows, 16), rows), :]

    def half(ref, which):
        return ref.at[pl.ds(pl.multiple_of(which * rows * chips, 16), rows * chips), :]

    def pair_copy(index, src, dst):
        return remote(src, dst, pair_send.at[index], pair_recv.at[index], other)

    def exchange_start(phase, src, dst):
        upper = chip >= chips // 2

        @pl.loop(0, chips)
        def _(step):
            j = jnp.where(upper, step, chips - 1 - step)

            @pl.when(j != chip)
            def _():
                remote(chunk(src, j), chunk(dst, chip), send_sem.at[phase, j], recv_sem.at[phase, chip], j * 2 + core).start()

        chunk(dst, chip)[...] = chunk(src, chip)[...]

    def exchange_wait(phase, src, dst):
        @pl.loop(1, chips)
        def _(step):
            j = lax.rem(chip + chips - step, chips)
            copy = remote(chunk(src, j), chunk(dst, j), send_sem.at[phase, j], recv_sem.at[phase, j], j * 2 + core)
            copy.wait_recv()
            copy.wait_send()

    def scan(src, dst, reverse):
        def step(i, total):
            at = chips - 1 - i if reverse else i
            chunk(dst, at)[...] = total.astype(BF16)
            return total + chunk(src, at)[...].astype(F32)

        lax.fori_loop(0, chips, step, jnp.zeros((rows, LANES), F32))

    def chip_sum(index, src, got, dst):
        copy = pair_copy(index, half(src, other_core), got)
        copy.wait_recv()
        copy.wait_send()
        dst[...] = (half(src, core)[...].astype(F32) + got[...].astype(F32)).astype(BF16)

    def share(index, base, src, got, out, dst, adds_first):
        sums = base[...].astype(F32)
        mine = half(src, core)[...].astype(F32)
        theirs = got[...].astype(F32)
        i_add = core == adds_first
        zero = jnp.zeros_like(sums)
        out[...] = (sums + jnp.where(i_add, zero, mine)).astype(BF16)
        pair_copy(index, out, half(dst, core)).start()
        half(dst, core)[...] = (sums + jnp.where(i_add, theirs, zero)).astype(BF16)

    def share_wait(index, out, dst):
        copy = pair_copy(index, out, half(dst, other_core))
        copy.wait_recv()
        copy.wait_send()

    kt = ktx.at[:, 128:384]
    vt = vtx.at[:, 128:384]
    turn(kt, k_ref)
    turn(vt, v_ref)
    if n * rows > PACKED:
        for ref in (state, dstate):
            ref[PACKED:, :] = jnp.zeros((n * rows - PACKED, LANES), BF16)

    @pl.loop(0, H // 4, unroll=True)
    def _(group):
        def one(h, i):
            phi = features(kt[qk_rows(h), :].astype(F32))
            return mm(vt[v_rows(h), :], phi, NT)

        put_state(state, group, heads4(group, one))

    first = me == 0
    end = me == n - 1
    after = jnp.minimum(me + 1, n - 1)
    before = jnp.maximum(me - 1, 0)
    pl.semaphore_wait(barrier, n - 1)

    def rim_copies(to):
        return [
            remote(k_ref.at[BLK - WIN :, :], kx.at[64:128, :], rim_send.at[0], rim_recv.at[0], to),
            remote(v_ref.at[BLK - WIN :, :], vx.at[64:128, :], rim_send.at[1], rim_recv.at[1], to),
        ]

    @pl.when(jnp.logical_not(end))
    def _():
        for copy in rim_copies(after):
            copy.start()

    pair_copy(0, half(state, other_core), pair1).start()
    turn(qt, q_ref)
    turn(dot, do_ref)
    chip_sum(0, state, pair1, sum1)
    exchange_start(0, sum1, got1)
    kx[0:64, :] = jnp.zeros((64, H * FD), BF16)
    kx[128:384, :] = k_ref[...]
    vx[0:64, :] = jnp.zeros((64, MAIN), BF16)
    vx[128:384, :] = v_ref[...]
    for c in range(MAIN // LANES):
        gain[c * LANES : (c + 1) * LANES, :] = jnp.broadcast_to(gain_in[c : c + 1, :], (LANES, LANES)).T

    @pl.when(first)
    def _():
        kx[64:128, :] = jnp.zeros((64, H * FD), BF16)
        vx[64:128, :] = jnp.zeros((64, MAIN), BF16)

    @pl.when(jnp.logical_not(first))
    def _():
        for copy in rim_copies(before):
            copy.wait_recv()

    @pl.when(jnp.logical_not(end))
    def _():
        for copy in rim_copies(after):
            copy.wait_send()

    turn(ktx.at[:, 0:128], kx.at[0:128, :])
    turn(vtx.at[:, 0:128], vx.at[0:128, :])
    stage_local(0, first, qt, dot, num, win, dq, dk, dv, kx, vx, ktx, vtx)
    exchange_wait(0, sum1, got1)
    scan(got1, send2, False)
    exchange_start(1, send2, base1)
    stage_local(1, first, qt, dot, num, win, dq, dk, dv, kx, vx, ktx, vtx)
    exchange_wait(1, send2, base1)
    share(1, base1, state, pair1, out1, prefix, 1)
    rim_out[0 : H * FD, :] = dk[:, 0:128].astype(BF16)
    rim_out[H * FD :, :] = dv[:, 0:128].astype(BF16)
    def rim_back(to):
        return remote(rim_out, rim_in, rim_send.at[2], rim_recv.at[2], to)

    @pl.when(jnp.logical_not(first))
    def _():
        rim_back(before).start()

    share_wait(1, out1, prefix)
    stage_mix(prefix, qt, dot, num, win, gain, dnum, dstate, outt)

    pair_copy(2, half(dstate, other_core), pair3).start()

    turn_out(out_ref, outt)
    chip_sum(2, dstate, pair3, sum3)
    exchange_start(2, sum3, got3)
    dkl = dk.at[:, 128:384]
    dvl = dv.at[:, 128:384]
    stage_back(0, prefix, qt, kt, k_ref, v_ref, dnum, dq, dkl, dvl, dqt)
    exchange_wait(2, sum3, got3)
    scan(got3, send4, True)
    exchange_start(3, send4, base3)
    stage_back(1, prefix, qt, kt, k_ref, v_ref, dnum, dq, dkl, dvl, dqt)
    exchange_wait(3, send4, base3)
    share(3, base3, dstate, pair3, out3, suffix, 0)
    turn_out(qg_ref, dqt)

    @pl.when(end)
    def _():
        rim_in[...] = jnp.zeros_like(rim_in)

    @pl.when(jnp.logical_not(end))
    def _():
        rim_back(after).wait_recv()

    @pl.when(jnp.logical_not(first))
    def _():
        rim_back(before).wait_send()

    share_wait(3, out3, suffix)
    stage_last(suffix, kt, vt, dkl, dvl, rim_in, dkt, dvt)


def turn_out(dst, src):
    for c in range(dst.shape[1] // LANES):
        cols = slice(c * LANES, (c + 1) * LANES)
        dst[:, cols] = src[cols, :].T.astype(BF16)


def finish(out_in, qg_in, dkt, dvt, out_ref, qg_ref, kg_ref, vg_ref):
    out_ref[...] = out_in[...]
    qg_ref[...] = qg_in[...]
    turn_out(kg_ref, dkt)
    turn_out(vg_ref, dvt)


def on_device(q, k, v, do, gain):
    n = lax.axis_size("seq")
    rows = -(-PACKED // (16 * n)) * 16
    chips = n // 2
    vm = pltpu.VMEM
    packed = vm((n * rows, LANES), BF16)
    qk, vv = (H * FD, BLK), (MAIN, BLK)
    outs = pl.pallas_call(
        functools.partial(whole, n, rows),
        out_shape=[jax.ShapeDtypeStruct(x.shape, BF16) for x in (do, q)] + [
            jax.ShapeDtypeStruct(s, BF16) for s in (qk, vv)],
        in_specs=[pl.BlockSpec(memory_space=vm)] * 5,
        out_specs=[pl.BlockSpec(memory_space=vm)] * 4,
        scratch_shapes=[packed] * 4 + [vm((chips * rows, LANES), BF16)] * 12 + [vm((H * FD + MAIN, LANES), BF16)] * 2 + [
            vm(qk, BF16), vm(vv, BF16), vm(vv, BF16), vm(vv, BF16), vm(vv, F32), vm(vv, F32),
            vm(qk, F32), vm((H * FD, 384), F32), vm((MAIN, 384), F32),
            vm(qk, F32),
            vm((384, H * FD), BF16), vm((384, MAIN), BF16), vm((H * FD, 384), BF16), vm((MAIN, 384), BF16),
            vm((MAIN, LANES), F32),
            pltpu.SemaphoreType.DMA((4, chips)), pltpu.SemaphoreType.DMA((4, chips)),
            pltpu.SemaphoreType.DMA((4,)), pltpu.SemaphoreType.DMA((4,)),
            pltpu.SemaphoreType.DMA((3,)), pltpu.SemaphoreType.DMA((3,)),
        ],
        compiler_params=pltpu.CompilerParams(
            vmem_limit_bytes=56 * 1024 * 1024, collective_id=0, has_side_effects=True),
    )(q, k, v, do, gain.reshape(MAIN // LANES, LANES))
    steps = 2
    whole_cols = [pl.BlockSpec((BLK, x // steps), lambda i: (0, i)) for x in (MAIN, H * FD, H * FD, MAIN)]
    turned = [pl.BlockSpec((x // steps, BLK), lambda i: (i, 0)) for x in (H * FD, MAIN)]
    return pl.pallas_call(
        finish,
        grid=(steps,),
        out_shape=[jax.ShapeDtypeStruct(x.shape, BF16) for x in (do, q, k, v)],
        in_specs=whole_cols[:2] + turned,
        out_specs=whole_cols,
    )(*outs)


def solution(mesh):
    split = P(("groups", "seq"), None)
    return jax.shard_map(
        on_device, mesh=mesh, in_specs=(split,) * 4 + (P(),), out_specs=(split,) * 4, check_vma=False
    )
```
